256 devices in a mesh: row: 16 (over y, x_lo, core), col: 16 (over x_hi, z).
Axes of the slice: x: 4 (x_hi: 2, x_lo: 2; x = x_hi * 2 + x_lo), y: 4, z: 8, core: 2. Of those that a mesh axis runs over, the one named last changes fastest.
Arguments:
- grads: bfloat16 [8192, 8192], P('row'), may hold values from -0.0625 to 0.0625
- seeds: int32 [8192], replicated, may hold values from 0 to 12
- bank: bfloat16 [256, 8192], P('row'), may hold values from -6 to 6
- query_ids: int32 [128], replicated, may hold values from 0 to 255, as said below
Outputs:
- solution: float32 [8192, 128], P('row')
- residual: float32 [8192, 128], P('row')
The draws below stay inside these ranges and needn't reach their ends.
Inputs may be any that keep to these rules, and one draw needn't show every extreme that they name: `query_ids`: the 128 ids are distinct.
All inputs are finite; a program needn't handle non-finite values.
Results may differ from the reference program's by a relative error of at most 0.0003.
Values may be sent and summed in bfloat16 or wider, within the bound.
No kernel may reach another device: no remote copies, remote signals or barrier semaphores. Data moves between devices by JAX's collectives and lax.ppermute only.
A program may use at most 128 MiB of HBM per device.

```python
import jax
import jax.numpy as jnp
from jax import lax

K = 8192
R = 128
ITERS = 2
N = 8192
QBANK = 256


def draw_query_ids(key, part):
    order = jax.random.permutation(jax.random.fold_in(key, 7), QBANK)
    return order[:R].astype(jnp.int32)


def set_ends(drawn, own_key, low, top_value):
    extent = drawn.shape
    place = [jax.random.randint(jax.random.fold_in(own_key, axis), (), 0, extent[axis]) for axis in range(len(extent))]
    drawn = drawn.at[tuple(place)].set(low)
    longest = extent.index(max(extent))
    place[longest] = (place[longest] + 1) % extent[longest]
    return drawn.at[tuple(place)].set(top_value)


def shard_levels(own_key, extent, pieces, low, top_value):
    def one(position, blocks):
        heights = jax.random.uniform(jax.random.fold_in(jax.random.fold_in(own_key, 6), position), (blocks,), jnp.float32, low / len(pieces), top_value / len(pieces))
        return jnp.repeat(jnp.exp(heights), extent[position] // blocks).reshape((-1,) + (1,) * (len(extent) - position - 1))

    loudness = one(*pieces[0])
    for cut in pieces[1:]:
        loudness = loudness * one(*cut)
    return loudness


def noise(stream_key, dims, spread, bound, shards=(), held_as=jnp.bfloat16):
    drawn = spread * jax.random.normal(stream_key, dims, jnp.float32)
    if shards:
        drawn = drawn * shard_levels(stream_key, dims, shards, -0.22, 0.18)
    return jnp.clip(drawn, -bound, bound).astype(held_as)


def setup_inputs(seed: int = 0) -> dict:
    key_of = jax.random.split(jax.random.key(seed), 5)
    return {
        "grads": noise(key_of[0], (N, K), K ** -0.5, 0.0625, ((0, 16),)),
        "seeds": set_ends(jax.random.randint(key_of[1], (N,), 0, 13), jax.random.fold_in(key_of[1], 1), 0, 12).astype(jnp.int32),
        "bank": noise(key_of[2], (QBANK, K), 1.0, 6.0, ((0, 16),)),
        "query_ids": draw_query_ids(jax.random.fold_in(key_of[4], 71), 0),
    }


damping = 0.5

def symmetric(mat):
    return 0.5 * (mat + mat.T)

def solve_spd(mat, right):
    factor = jnp.linalg.cholesky(mat)
    return jax.scipy.linalg.cho_solve((factor, True), right)

def inner(left, right):
    return lax.dot_general(left.astype(jnp.float32), right.astype(jnp.float32), (((0,), (0,)), ((), ())), precision=lax.Precision.HIGHEST, preferred_element_type=jnp.float32)

def reference(grads, seeds, bank, query_ids):
    scale = jnp.exp2(seeds.astype(jnp.float32) / 4.0)
    chosen = bank[query_ids]
    rhs = scale[:, None] * lax.dot_general(grads.astype(jnp.float32), chosen.astype(jnp.float32), (((1,), (1,)), ((), ())), preferred_element_type=jnp.float32)
    wide = grads.astype(jnp.float32)
    gram = scale[:, None] * jnp.dot(wide, wide.T, precision=lax.Precision.HIGHEST) * scale[None, :]
    solution = jnp.zeros_like(rhs)
    residual = rhs
    direction = rhs
    norm_now = inner(residual, residual)
    for step in range(ITERS):
        image = jnp.dot(gram, direction, precision=lax.Precision.HIGHEST) + damping * direction
        curv = symmetric(inner(direction, image))
        alpha = solve_spd(curv, norm_now)
        solution = solution + jnp.dot(direction, alpha, precision=lax.Precision.HIGHEST)
        residual = residual - jnp.dot(image, alpha, precision=lax.Precision.HIGHEST)
        if step + 1 < ITERS:
            fresh = inner(residual, residual)
            beta = solve_spd(symmetric(norm_now), fresh)
            direction = residual + jnp.dot(direction, beta, precision=lax.Precision.HIGHEST)
            norm_now = fresh
    return (solution, residual)
```

```python
import jax
import jax.numpy as jnp
from jax import lax
from jax.sharding import PartitionSpec as P

damping = 0.5


def symmetric(mat):
    return 0.5 * (mat + mat.T)


def solve_spd(mat, right):
    factor = jnp.linalg.cholesky(mat)
    return jax.scipy.linalg.cho_solve((factor, True), right)


def full(left, right, dims=((1,), (0,))):
    return lax.dot_general(
        left,
        right,
        (dims, ((), ())),
        precision=lax.Precision.HIGHEST,
        preferred_element_type=jnp.float32,
    )


def two_terms(value):
    high = lax.reduce_precision(value, 8, 7)
    return jnp.concatenate([high, value - high]).astype(jnp.bfloat16)


def swap(pieces, axis):
    return lax.all_to_all(pieces, axis, 0, 0, tiled=True)


def spread(piece, axis, size):
    return swap(jnp.broadcast_to(piece[None], (size,) + piece.shape), axis)


def split_last(value, parts):
    lead, last = value.shape
    return value.reshape(lead, parts, last // parts).transpose(1, 0, 2)


def join_last(pieces):
    parts, lead, last = pieces.shape
    return pieces.transpose(1, 0, 2).reshape(lead, parts * last)


def on_device(rows_n, cols_n, grads, seeds, bank, query_ids):
    rows, depth = grads.shape
    queries = query_ids.shape[0]
    mine = queries // cols_n
    my_row = lax.axis_index("row")
    my_col = lax.axis_index("col")
    own_seeds = lax.dynamic_slice_in_dim(seeds, my_row * rows, rows)
    scale = jnp.exp2(own_seeds.astype(jnp.float32) / 4.0)[None, :]

    def project(value):
        both = lax.dot_general(
            two_terms(value), grads, (((1,), (1,)), ((), ())), preferred_element_type=jnp.float32
        )
        return scale * (both[:mine] + both[mine:])

    def gather_back(value):
        both = lax.dot_general(
            two_terms(scale * value), grads, (((1,), (0,)), ((), ())), preferred_element_type=jnp.float32
        )
        part = both[:mine] + both[mine:]
        piece = jnp.sum(swap(split_last(part, rows_n), "row"), axis=0)
        return join_last(spread(piece, "row", rows_n))

    bank_rows = bank.shape[0]
    ids = lax.dynamic_slice_in_dim(query_ids, my_col * mine, mine) - my_row * bank_rows
    selector = (ids[:, None] == jnp.arange(bank_rows, dtype=jnp.int32)[None, :]).astype(jnp.bfloat16)
    picked = jnp.dot(selector, bank, preferred_element_type=jnp.float32).astype(jnp.bfloat16)
    arrived = swap(split_last(picked, rows_n), "row").astype(jnp.float32)
    piece = jnp.sum(arrived, axis=0).astype(jnp.bfloat16)
    chosen = join_last(spread(piece, "row", rows_n))

    base = scale * lax.dot_general(
        chosen, grads, (((1,), (1,)), ((), ())), preferred_element_type=jnp.float32
    )
    back = gather_back(base)
    wide = chosen.astype(jnp.float32)
    square = jnp.sum(wide * back, axis=1, keepdims=True)
    curve = jnp.sum(back * back, axis=1, keepdims=True) + damping * square
    step = square / curve
    other = base - step * (project(back) + damping * base)
    other_image = project(gather_back(other)) + damping * other

    lanes = 128
    message = jnp.concatenate(
        [base, other, other_image, jnp.broadcast_to(step, (mine, lanes))], axis=1
    )
    held = spread(message, "col", cols_n).reshape(queries, 3 * rows + lanes)
    base, other, other_image = held[:, :rows], held[:, rows : 2 * rows], held[:, 2 * rows : 3 * rows]
    step = held[:, 3 * rows]

    last = ((1,), (1,))
    moments = jnp.concatenate(
        [
            full(base, base, last),
            full(base, other, last),
            full(other, other, last),
            full(other, other_image, last),
        ]
    )
    piece = jnp.sum(swap(moments.reshape(rows_n, -1, queries), "row"), axis=0)
    moments = spread(piece, "row", rows_n).reshape(4, queries, queries)
    bb, bt, tt, tat = moments[0], moments[1], moments[2], symmetric(moments[3])

    bab = symmetric((bb - bt) / step[None, :])
    tab = (bt.T - tt) / step[None, :]
    alpha = solve_spd(bab, bb)
    second = alpha / step[:, None]
    first = jnp.eye(queries, dtype=jnp.float32) - second

    def quad(left, a, b, c, right):
        cross = full(left.T, full(b, right))
        return full(left.T, full(a, left)) + cross + cross.T + full(right.T, full(c, right))

    fresh = quad(first, bb, bt, tt, second)
    beta = solve_spd(symmetric(bb), fresh)
    mixed = first + beta
    curv = symmetric(quad(mixed, bab, tab.T, tat, second))
    alpha_next = solve_spd(curv, fresh)
    gain = full(mixed, alpha_next)
    gain_other = full(second, alpha_next)
    shift = gain / step[:, None]
    lead = ((0,), (0,))
    solution = full(base, alpha + gain, lead) + full(other, gain_other, lead)
    residual = (
        full(base, first - shift, lead)
        + full(other, second + shift, lead)
        - full(other_image, gain_other, lead)
    )
    return (solution, residual)


def solution(mesh):
    placed = (P("row", None), P(), P("row", None), P())

    def body(*args):
        return on_device(mesh.shape["row"], mesh.shape["col"], *args)

    return jax.shard_map(
        body,
        mesh=mesh,
        in_specs=placed,
        out_specs=(P("row", None), P("row", None)),
        check_vma=False,
    )
```

```python
import functools

import jax
import jax.numpy as jnp
from jax import lax
from jax.experimental import pallas as pl
from jax.experimental.pallas import tpu as pltpu
from jax.sharding import PartitionSpec as P

damping = 0.5


def full(left, right, dims=((1,), (0,))):
    return lax.dot_general(
        left,
        right,
        (dims, ((), ())),
        precision=lax.Precision.HIGHEST,
        preferred_element_type=jnp.float32,
    )


def two_terms(value):
    high = lax.reduce_precision(value, 8, 7)
    return jnp.concatenate([high, value - high]).astype(jnp.bfloat16)


def swap(pieces, axis):
    return lax.all_to_all(pieces, axis, 0, 0, tiled=True)


def spread(piece, axis, size):
    return swap(jnp.broadcast_to(piece[None], (size,) + piece.shape), axis)


def split_last(value, parts):
    lead, last = value.shape
    return value.reshape(lead, parts, last // parts).transpose(1, 0, 2)


def join_last(pieces):
    parts, lead, last = pieces.shape
    return pieces.transpose(1, 0, 2).reshape(lead, parts * last)


def moments_kernel(rows, held_ref, out_ref):
    base = held_ref[:, :rows]
    other = held_ref[:, rows : 2 * rows]
    image = held_ref[:, 2 * rows : 3 * rows]
    queries = base.shape[0]
    last = ((1,), (1,))
    out_ref[:queries] = full(base, base, last)
    out_ref[queries : 2 * queries] = full(other, base, last)
    out_ref[2 * queries : 3 * queries] = full(other, other, last)
    out_ref[3 * queries :] = full(other, image, last)


def moments_of(held, rows):
    queries = held.shape[0]
    return pl.pallas_call(
        functools.partial(moments_kernel, rows),
        out_shape=jax.ShapeDtypeStruct((4 * queries, queries), jnp.float32),
    )(held)


def reduce_moments(moments, rows_n):
    queries = moments.shape[1]
    piece = jnp.sum(swap(moments.reshape(rows_n, -1, queries), "row"), axis=0)
    return spread(piece, "row", rows_n).reshape(4 * queries, queries)


def inverse_spd(mat, eye, inv_ref, left_ref):
    on_diag = mat * eye
    across = lax.rsqrt(jnp.sum(on_diag, axis=0, keepdims=True))
    down = lax.rsqrt(jnp.sum(on_diag, axis=1, keepdims=True))
    unit = mat * across * down
    reach = jnp.sum(jnp.abs(unit), axis=1, keepdims=True)
    share = 1.0 / jnp.max(reach, axis=0, keepdims=True)
    left = eye - share * unit
    inv = share * (eye + left)
    left = full(left, left)
    for _ in range(4):
        inv, left = inv + full(inv, left), full(left, left)
    inv_ref[...] = inv
    left_ref[...] = left

    def open_still(state):
        count, size = state
        return jnp.logical_and(count < 40, size > 1e-5)

    def again(state):
        inv, left = inv_ref[...], left_ref[...]
        inv_ref[...] = inv + full(inv, left)
        left = full(left, left)
        left_ref[...] = left
        return state[0] + 1, jnp.sum(left * left)

    lax.while_loop(open_still, again, (0, jnp.sum(left * left)))
    inv = inv_ref[...]
    inv = inv + full(inv, left_ref[...])
    return inv * across * down


def solve_with(mat, inv, right):
    first = full(inv, right)
    return first + full(inv, right - full(mat, first))


def finish_kernel(rows, held_ref, moments_ref, solution_ref, residual_ref, inv_ref, left_ref):
    queries = held_ref.shape[0]
    bb = moments_ref[:queries]
    tb = moments_ref[queries : 2 * queries]
    tt = moments_ref[2 * queries : 3 * queries]
    tat = moments_ref[3 * queries :]
    per_step = 1.0 / held_ref[:, 3 * rows :]
    shape = (queries, queries)
    row_id = lax.broadcasted_iota(jnp.int32, shape, 0)
    eye = jnp.where(row_id == lax.broadcasted_iota(jnp.int32, shape, 1), 1.0, 0.0)

    bab = per_step * (bb - tb)
    bat = per_step * (tb.T - tt)
    tab = bat.T
    inv = inverse_spd(bab, eye, inv_ref, left_ref)
    alpha = solve_with(bab, inv, bb)
    second = per_step * alpha
    second_t = second.T
    first = eye - second
    fresh = full(second_t, tb - full(tab, alpha))
    mixed = -solve_with(bab, inv, full(bat, second))
    curv = full(second_t, full(tab, mixed) + full(tat, second))
    curv = 0.5 * (curv + curv.T)
    inv = inverse_spd(curv, eye, inv_ref, left_ref)
    alpha_next = solve_with(curv, inv, fresh)
    gain = full(mixed, alpha_next)
    gain_other = full(second, alpha_next)
    shift = per_step * gain

    base = held_ref[:, :rows].T
    other = held_ref[:, rows : 2 * rows].T
    image = held_ref[:, 2 * rows : 3 * rows].T
    solution_ref[...] = full(base, alpha + gain) + full(other, gain_other)
    residual_ref[...] = full(base, first - shift) + full(other, second + shift) - full(image, gain_other)


def finish(held, moments, rows):
    queries = held.shape[0]
    shape = jax.ShapeDtypeStruct((rows, queries), jnp.float32)
    return pl.pallas_call(
        functools.partial(finish_kernel, rows),
        out_shape=(shape, shape),
        scratch_shapes=[pltpu.VMEM((queries, queries), jnp.float32)] * 2,
    )(held, moments)


def on_device(rows_n, cols_n, grads, seeds, bank, query_ids):
    rows, depth = grads.shape
    queries = query_ids.shape[0]
    mine = queries // cols_n
    my_row = lax.axis_index("row")
    my_col = lax.axis_index("col")
    own_seeds = lax.dynamic_slice_in_dim(seeds, my_row * rows, rows)
    scale = jnp.exp2(own_seeds.astype(jnp.float32) / 4.0)[None, :]

    def project(value):
        both = lax.dot_general(
            two_terms(value), grads, (((1,), (1,)), ((), ())), preferred_element_type=jnp.float32
        )
        return scale * (both[:mine] + both[mine:])

    def gather_back(value):
        both = lax.dot_general(
            two_terms(scale * value), grads, (((1,), (0,)), ((), ())), preferred_element_type=jnp.float32
        )
        part = both[:mine] + both[mine:]
        piece = jnp.sum(swap(split_last(part, rows_n), "row"), axis=0)
        return join_last(spread(piece, "row", rows_n))

    bank_rows = bank.shape[0]
    ids = lax.dynamic_slice_in_dim(query_ids, my_col * mine, mine) - my_row * bank_rows
    selector = (ids[:, None] == jnp.arange(bank_rows, dtype=jnp.int32)[None, :]).astype(jnp.bfloat16)
    picked = jnp.dot(selector, bank, preferred_element_type=jnp.float32).astype(jnp.bfloat16)
    arrived = swap(split_last(picked, rows_n), "row").astype(jnp.float32)
    piece = jnp.sum(arrived, axis=0).astype(jnp.bfloat16)
    chosen = join_last(spread(piece, "row", rows_n))

    base = scale * lax.dot_general(
        chosen, grads, (((1,), (1,)), ((), ())), preferred_element_type=jnp.float32
    )
    back = gather_back(base)
    wide = chosen.astype(jnp.float32)
    square = jnp.sum(wide * back, axis=1, keepdims=True)
    curve = jnp.sum(back * back, axis=1, keepdims=True) + damping * square
    step = square / curve
    other = base - step * (project(back) + damping * base)
    other_image = project(gather_back(other)) + damping * other

    lanes = 128
    message = jnp.concatenate(
        [base, other, other_image, jnp.broadcast_to(step, (mine, lanes))], axis=1
    )
    held = spread(message, "col", cols_n).reshape(queries, 3 * rows + lanes)
    return finish(held, reduce_moments(moments_of(held, rows), rows_n), rows)


def solution(mesh):
    placed = (P("row", None), P(), P("row", None), P())

    def body(*args):
        return on_device(mesh.shape["row"], mesh.shape["col"], *args)

    return jax.shard_map(
        body,
        mesh=mesh,
        in_specs=placed,
        out_specs=(P("row", None), P("row", None)),
        check_vma=False,
    )
```

```python
import functools

import jax
import jax.numpy as jnp
from jax import lax
from jax.experimental import pallas as pl
from jax.experimental.pallas import tpu as pltpu
from jax.sharding import PartitionSpec as P

damping = 0.5


def full(left, right, dims=((1,), (0,))):
    return lax.dot_general(
        left,
        right,
        (dims, ((), ())),
        precision=lax.Precision.HIGHEST,
        preferred_element_type=jnp.float32,
    )


def two_terms(value):
    high = value.astype(jnp.bfloat16).astype(jnp.float32)
    return jnp.concatenate([high, value - high]).astype(jnp.bfloat16)


def both_terms(product):
    half = product.shape[0] // 2
    return product[:half] + product[half:]


def bf16_dot(left, right, right_dim):
    return lax.dot_general(
        left, right, (((1,), (right_dim,)), ((), ())), preferred_element_type=jnp.float32
    )


def swap(pieces, axis):
    return lax.all_to_all(pieces, axis, 0, 0, tiled=True)


def spread(piece, axis, size):
    return swap(jnp.broadcast_to(piece[None], (size,) + piece.shape), axis)


def inverse_spd(mat, eye, inv_ref, left_ref):
    on_diag = mat * eye
    across = lax.rsqrt(jnp.sum(on_diag, axis=0, keepdims=True))
    down = lax.rsqrt(jnp.sum(on_diag, axis=1, keepdims=True))
    unit = mat * across * down
    reach = jnp.sum(jnp.abs(unit), axis=1, keepdims=True)
    share = 1.0 / jnp.max(reach, axis=0, keepdims=True)
    left = eye - share * unit
    inv = share * (eye + left)
    left = full(left, left)
    for _ in range(4):
        inv, left = inv + full(inv, left), full(left, left)
    inv_ref[...] = inv
    left_ref[...] = left

    def open_still(state):
        count, size = state
        return jnp.logical_and(count < 40, size > 1e-5)

    def again(state):
        inv, left = inv_ref[...], left_ref[...]
        inv_ref[...] = inv + full(inv, left)
        left = full(left, left)
        left_ref[...] = left
        return state[0] + 1, jnp.sum(left * left)

    lax.while_loop(open_still, again, (0, jnp.sum(left * left)))
    inv = inv_ref[...]
    inv = inv + full(inv, left_ref[...])
    return inv * across * down


def solve_with(mat, inv, right):
    first = full(inv, right)
    return first + full(inv, right - full(mat, first))


def pick_kernel(cols_n, ids_ref, seeds_ref, bank_ref, picked_ref, scale_ref):
    parts, mine, width = picked_ref.shape
    bank_rows = bank_ref.shape[0]
    my_row = lax.axis_index("row")
    my_col = lax.axis_index("col")
    query = lax.broadcasted_iota(jnp.int32, (mine, bank_rows), 0)
    held = lax.broadcasted_iota(jnp.int32, (mine, bank_rows), 1)
    chosen = jnp.zeros((mine, bank_rows), jnp.bool_)
    for q in range(mine):
        local = ids_ref[my_col * mine + q] - my_row * bank_rows
        chosen = jnp.logical_or(chosen, jnp.logical_and(query == q, held == local))
    selector = jnp.where(chosen, 1.0, 0.0).astype(jnp.bfloat16)
    for k in range(parts):
        picked = bf16_dot(selector, bank_ref[:, k * width : (k + 1) * width], 0)
        picked_ref[k] = picked.astype(jnp.bfloat16)
    lanes = seeds_ref.shape[1]
    groups = scale_ref.shape[1] // lanes
    for k in range(groups):
        seeds = seeds_ref[pl.ds(my_row * groups + k, 1), :]
        scale_ref[:, k * lanes : (k + 1) * lanes] = jnp.exp2(seeds.astype(jnp.float32) / 4.0)


def sum_kernel(parts_ref, out_ref):
    total = parts_ref[0].astype(jnp.float32)
    for k in range(1, parts_ref.shape[0]):
        total += parts_ref[k].astype(jnp.float32)
    for k in range(out_ref.shape[0]):
        out_ref[k] = total.astype(out_ref.dtype)


def late_kernel(parts_ref, image_ref, out_ref):
    total = parts_ref[0]
    for k in range(1, parts_ref.shape[0]):
        total += parts_ref[k]
    late = jnp.concatenate([image_ref[...], total], axis=1)
    for k in range(out_ref.shape[0]):
        out_ref[k] = late


def partial_back(value, grads_ref, part_ref):
    terms = two_terms(value)
    parts, _, width = part_ref.shape
    for k in range(parts):
        product = bf16_dot(terms, grads_ref[:, k * width : (k + 1) * width], 0)
        part_ref[k] = both_terms(product)


def base_kernel(chosen_ref, scale_ref, grads_ref, base_ref, part_ref):
    parts, _, width = chosen_ref.shape
    total = jnp.zeros(base_ref.shape, jnp.float32)
    for k in range(parts):
        total += bf16_dot(chosen_ref[k], grads_ref[:, k * width : (k + 1) * width], 1)
    scale = scale_ref[...]
    base = scale * total
    base_ref[...] = base
    partial_back(scale * base, grads_ref, part_ref)


def project(back_ref, grads_ref):
    parts, lead, width = back_ref.shape
    total = jnp.zeros((2 * lead, grads_ref.shape[0]), jnp.float32)
    for k in range(parts):
        total += bf16_dot(two_terms(back_ref[k]), grads_ref[:, k * width : (k + 1) * width], 1)
    return both_terms(total)


def other_kernel(back_ref, chosen_ref, base_ref, scale_ref, grads_ref, message_ref, part_ref):
    parts, lead, width = back_ref.shape
    rows = base_ref.shape[1]
    square = jnp.zeros((lead, width), jnp.float32)
    curve = jnp.zeros((lead, width), jnp.float32)
    for k in range(parts):
        back = back_ref[k]
        square += chosen_ref[k].astype(jnp.float32) * back
        curve += back * back
    square = jnp.sum(square, axis=1, keepdims=True)
    curve = jnp.sum(curve, axis=1, keepdims=True)
    step = square / (curve + damping * square)
    base = base_ref[...]
    scale = scale_ref[...]
    other = base - step * (scale * project(back_ref, grads_ref) + damping * base)
    message_ref[:, :rows] = base
    message_ref[:, rows : 2 * rows] = other
    message_ref[:, 2 * rows :] = jnp.broadcast_to(step, (lead, message_ref.shape[1] - 2 * rows))
    partial_back(scale * other, grads_ref, part_ref)


def image_kernel(back_ref, message_ref, held_ref, scale_ref, grads_ref, image_ref, moments_ref):
    rows = image_ref.shape[1]
    queries = held_ref.shape[0]
    own_base = message_ref[:, :rows]
    own_other = message_ref[:, rows : 2 * rows]
    image = scale_ref[...] * project(back_ref, grads_ref) + damping * own_other
    image_ref[...] = image
    base = held_ref[:, :rows]
    other = held_ref[:, rows : 2 * rows]
    last = ((1,), (1,))
    moments_ref[:, :queries] = full(own_base, base, last)
    moments_ref[:, queries : 2 * queries] = full(own_other, base, last)
    moments_ref[:, 2 * queries : 3 * queries] = full(own_other, other, last)
    moments_ref[:, 3 * queries :] = full(image, other, last)


def finish_kernel(rows, held_ref, late_ref, solution_ref, residual_ref, inv_ref, left_ref):
    queries = held_ref.shape[0]
    bb = late_ref[:, rows : rows + queries]
    tb = late_ref[:, rows + queries : rows + 2 * queries]
    tt = late_ref[:, rows + 2 * queries : rows + 3 * queries]
    tat = late_ref[:, rows + 3 * queries :]
    per_step = 1.0 / held_ref[:, 2 * rows :]
    shape = (queries, queries)
    row_id = lax.broadcasted_iota(jnp.int32, shape, 0)
    eye = jnp.where(row_id == lax.broadcasted_iota(jnp.int32, shape, 1), 1.0, 0.0)

    bab = per_step * (bb - tb)
    bat = per_step * (tb.T - tt)
    tab = bat.T
    inv = inverse_spd(bab, eye, inv_ref, left_ref)
    alpha = solve_with(bab, inv, bb)
    second = per_step * alpha
    second_t = second.T
    first = eye - second
    fresh = full(second_t, tb - full(tab, alpha))
    mixed = -solve_with(bab, inv, full(bat, second))
    curv = full(second_t, full(tab, mixed) + full(tat, second))
    curv = 0.5 * (curv + curv.T)
    inv = inverse_spd(curv, eye, inv_ref, left_ref)
    alpha_next = solve_with(curv, inv, fresh)
    gain = full(mixed, alpha_next)
    gain_other = full(second, alpha_next)
    shift = per_step * gain

    base = held_ref[:, :rows].T
    other = held_ref[:, rows : 2 * rows].T
    image = late_ref[:, :rows].T
    solution_ref[...] = full(base, alpha + gain) + full(other, gain_other)
    residual_ref[...] = full(base, first - shift) + full(other, second + shift) - full(image, gain_other)


def call(kernel, shapes, *args, scratch=(), first=pltpu.VMEM, dtype=jnp.float32, limit=8):
    shapes = [(shape, dtype if k == 0 else jnp.float32) for k, shape in enumerate(shapes)]
    spaces = [first] + [pltpu.VMEM] * (len(args) - 1)
    outs = pl.pallas_call(
        kernel,
        out_shape=tuple(jax.ShapeDtypeStruct(*shape) for shape in shapes),
        in_specs=[pl.BlockSpec(memory_space=space) for space in spaces],
        out_specs=tuple(pl.BlockSpec(memory_space=pltpu.VMEM) for _ in shapes),
        scratch_shapes=scratch,
        compiler_params=pltpu.CompilerParams(vmem_limit_bytes=limit * 2**20),
    )(*args)
    return outs if len(outs) > 1 else outs[0]


def on_device(rows_n, cols_n, grads, seeds, bank, query_ids):
    rows, depth = grads.shape
    queries = query_ids.shape[0]
    mine = queries // cols_n
    lanes = 128
    pieces = (rows_n, mine, depth // rows_n)

    def reduce_row(part):
        total = call(sum_kernel, [part.shape], swap(part, "row"), dtype=part.dtype)
        return swap(total, "row")

    picked, scale = call(
        functools.partial(pick_kernel, cols_n),
        [pieces, (1, rows)],
        query_ids,
        seeds.reshape(-1, lanes),
        bank,
        first=pltpu.SMEM,
        dtype=jnp.bfloat16,
    )
    chosen = reduce_row(picked)
    base, part = call(base_kernel, [(mine, rows), pieces], chosen, scale, grads)
    back = reduce_row(part)
    wide = 2 * rows + lanes
    message, part = call(other_kernel, [(mine, wide), pieces], back, chosen, base, scale, grads)
    held = spread(message, "col", cols_n).reshape(queries, wide)
    back = reduce_row(part)
    image, moments = call(
        image_kernel, [(mine, rows), (mine, 4 * queries)], back, message, held, scale, grads
    )
    late = (cols_n, mine, rows + 4 * queries)
    late = swap(call(late_kernel, [late], spread(moments, "row", rows_n), image), "col")
    square = pltpu.VMEM((queries, queries), jnp.float32)
    return call(
        functools.partial(finish_kernel, rows),
        [(rows, queries), (rows, queries)],
        held,
        late.reshape(queries, rows + 4 * queries),
        scratch=[square, square],
    )


def solution(mesh):
    placed = (P("row", None), P(), P("row", None), P())

    def body(*args):
        return on_device(mesh.shape["row"], mesh.shape["col"], *args)

    return jax.shard_map(
        body,
        mesh=mesh,
        in_specs=placed,
        out_specs=(P("row", None), P("row", None)),
        check_vma=False,
    )
```

```python
import functools

import jax
import jax.numpy as jnp
from jax import lax
from jax.experimental import pallas as pl
from jax.experimental.pallas import tpu as pltpu
from jax.sharding import PartitionSpec as P

damping = 0.5


def full(left, right, dims=((1,), (0,))):
    return lax.dot_general(
        left,
        right,
        (dims, ((), ())),
        precision=lax.Precision.HIGHEST,
        preferred_element_type=jnp.float32,
    )


def two_terms(value):
    high = value.astype(jnp.bfloat16).astype(jnp.float32)
    return jnp.concatenate([high, value - high]).astype(jnp.bfloat16)


def both_terms(product):
    half = product.shape[0] // 2
    return product[:half] + product[half:]


def bf16_dot(left, right, right_dim):
    return lax.dot_general(
        left, right, (((1,), (right_dim,)), ((), ())), preferred_element_type=jnp.float32
    )


def swap(pieces, axis):
    return lax.all_to_all(pieces, axis, 0, 0, tiled=True)


def spread(piece, axis, size):
    return swap(jnp.broadcast_to(piece[None], (size,) + piece.shape), axis)


def inverse_spd(mat, eye, inv_ref, left_ref):
    on_diag = mat * eye
    across = lax.rsqrt(jnp.sum(on_diag, axis=0, keepdims=True))
    down = lax.rsqrt(jnp.sum(on_diag, axis=1, keepdims=True))
    unit = mat * across * down
    reach = jnp.sum(jnp.abs(unit), axis=1, keepdims=True)
    share = 1.0 / jnp.max(reach, axis=0, keepdims=True)
    left = eye - share * unit
    inv = share * (eye + left)
    left = full(left, left)
    for _ in range(4):
        inv, left = inv + full(inv, left), full(left, left)
    inv_ref[...] = inv
    left_ref[...] = left

    def open_still(state):
        count, size = state
        return jnp.logical_and(count < 40, size > 1e-5)

    def again(state):
        inv, left = inv_ref[...], left_ref[...]
        inv_ref[...] = inv + full(inv, left)
        left = full(left, left)
        left_ref[...] = left
        return state[0] + 1, jnp.sum(left * left)

    lax.while_loop(open_still, again, (0, jnp.sum(left * left)))
    inv = inv_ref[...]
    inv = inv + full(inv, left_ref[...])
    return inv * across * down


def solve_with(mat, inv, right):
    first = full(inv, right)
    return first + full(inv, right - full(mat, first))


def pick_kernel(
    cols_n, ids_hbm, seeds_hbm, bank_hbm, picked_ref, scale_ref, ids_ref, seeds_ref, bank_ref, sems
):
    copies = [
        pltpu.make_async_copy(source, target, sems.at[k])
        for k, (source, target) in enumerate(
            [(ids_hbm, ids_ref), (bank_hbm, bank_ref), (seeds_hbm, seeds_ref)]
        )
    ]
    for copy in copies:
        copy.start()
    parts, mine, width = picked_ref.shape
    bank_rows = bank_ref.shape[0]
    my_row = lax.axis_index("row")
    my_col = lax.axis_index("col")
    query = lax.broadcasted_iota(jnp.int32, (mine, bank_rows), 0)
    held = lax.broadcasted_iota(jnp.int32, (mine, bank_rows), 1)
    chosen = jnp.zeros((mine, bank_rows), jnp.bool_)
    copies[0].wait()
    for q in range(mine):
        local = ids_ref[my_col * mine + q] - my_row * bank_rows
        chosen = jnp.logical_or(chosen, jnp.logical_and(query == q, held == local))
    selector = jnp.where(chosen, 1.0, 0.0).astype(jnp.bfloat16)
    copies[1].wait()
    for k in range(parts):
        picked = bf16_dot(selector, bank_ref[:, k * width : (k + 1) * width], 0)
        picked_ref[k] = picked.astype(jnp.bfloat16)
    lanes = seeds_ref.shape[1]
    groups = scale_ref.shape[1] // lanes
    copies[2].wait()
    for k in range(groups):
        seeds = seeds_ref[pl.ds(my_row * groups + k, 1), :]
        scale_ref[:, k * lanes : (k + 1) * lanes] = jnp.exp2(seeds.astype(jnp.float32) / 4.0)


def sum_kernel(parts_ref, out_ref):
    total = parts_ref[0].astype(jnp.float32)
    for k in range(1, parts_ref.shape[0]):
        total += parts_ref[k].astype(jnp.float32)
    for k in range(out_ref.shape[0]):
        out_ref[k] = total.astype(out_ref.dtype)


def late_kernel(parts_ref, image_ref, out_ref):
    total = parts_ref[0]
    for k in range(1, parts_ref.shape[0]):
        total += parts_ref[k]
    late = jnp.concatenate([image_ref[...], total], axis=1)
    for k in range(out_ref.shape[0]):
        out_ref[k] = late


def partial_back(value, grads_ref, part_ref):
    terms = two_terms(value)
    parts, _, width = part_ref.shape
    for k in range(parts):
        product = bf16_dot(terms, grads_ref[:, k * width : (k + 1) * width], 0)
        part_ref[k] = both_terms(product)


def base_kernel(chosen_ref, scale_ref, grads_hbm, base_ref, part_ref, grads_ref, sems):
    parts, lead, width = chosen_ref.shape
    copies = []
    for k in range(parts):
        block = (slice(None), pl.ds(k * width, width))
        copies.append(pltpu.make_async_copy(grads_hbm.at[block], grads_ref.at[block], sems.at[k]))
        copies[k].start()
    total = jnp.zeros(base_ref.shape, jnp.float32)
    for k in range(parts):
        copies[k].wait()
        total += bf16_dot(chosen_ref[k], grads_ref[:, k * width : (k + 1) * width], 1)
    scale = scale_ref[...]
    base = scale * total
    base_ref[...] = base
    partial_back(scale * base, grads_ref, part_ref)


def project(back_ref, grads_ref):
    parts, lead, width = back_ref.shape
    total = jnp.zeros((2 * lead, grads_ref.shape[0]), jnp.float32)
    for k in range(parts):
        total += bf16_dot(two_terms(back_ref[k]), grads_ref[:, k * width : (k + 1) * width], 1)
    return both_terms(total)


def other_kernel(back_ref, chosen_ref, base_ref, scale_ref, grads_ref, message_ref, part_ref):
    parts, lead, width = back_ref.shape
    rows = base_ref.shape[1]
    square = jnp.zeros((lead, width), jnp.float32)
    curve = jnp.zeros((lead, width), jnp.float32)
    for k in range(parts):
        back = back_ref[k]
        square += chosen_ref[k].astype(jnp.float32) * back
        curve += back * back
    square = jnp.sum(square, axis=1, keepdims=True)
    curve = jnp.sum(curve, axis=1, keepdims=True)
    step = square / (curve + damping * square)
    base = base_ref[...]
    scale = scale_ref[...]
    other = base - step * (scale * project(back_ref, grads_ref) + damping * base)
    message_ref[:, :rows] = base
    message_ref[:, rows : 2 * rows] = other
    message_ref[:, 2 * rows :] = jnp.broadcast_to(step, (lead, message_ref.shape[1] - 2 * rows))
    partial_back(scale * other, grads_ref, part_ref)


def image_kernel(back_ref, message_ref, held_ref, scale_ref, grads_ref, image_ref, moments_ref):
    rows = image_ref.shape[1]
    queries = held_ref.shape[0]
    own_base = message_ref[:, :rows]
    own_other = message_ref[:, rows : 2 * rows]
    image = scale_ref[...] * project(back_ref, grads_ref) + damping * own_other
    image_ref[...] = image
    base = held_ref[:, :rows]
    other = held_ref[:, rows : 2 * rows]
    last = ((1,), (1,))
    moments_ref[:, :queries] = full(own_base, base, last)
    moments_ref[:, queries : 2 * queries] = full(own_other, base, last)
    moments_ref[:, 2 * queries : 3 * queries] = full(own_other, other, last)
    moments_ref[:, 3 * queries :] = full(image, other, last)


def finish_kernel(rows, held_ref, late_ref, solution_ref, residual_ref, inv_ref, left_ref):
    queries = held_ref.shape[0]
    bb = late_ref[:, rows : rows + queries]
    tb = late_ref[:, rows + queries : rows + 2 * queries]
    tt = late_ref[:, rows + 2 * queries : rows + 3 * queries]
    tat = late_ref[:, rows + 3 * queries :]
    per_step = 1.0 / held_ref[:, 2 * rows :]
    shape = (queries, queries)
    row_id = lax.broadcasted_iota(jnp.int32, shape, 0)
    eye = jnp.where(row_id == lax.broadcasted_iota(jnp.int32, shape, 1), 1.0, 0.0)

    bab = per_step * (bb - tb)
    bat = per_step * (tb.T - tt)
    tab = bat.T
    inv = inverse_spd(bab, eye, inv_ref, left_ref)
    alpha = solve_with(bab, inv, bb)
    second = per_step * alpha
    second_t = second.T
    first = eye - second
    fresh = full(second_t, tb - full(tab, alpha))
    mixed = -solve_with(bab, inv, full(bat, second))
    curv = full(second_t, full(tab, mixed) + full(tat, second))
    curv = 0.5 * (curv + curv.T)
    inv = inverse_spd(curv, eye, inv_ref, left_ref)
    alpha_next = solve_with(curv, inv, fresh)
    gain = full(mixed, alpha_next)
    gain_other = full(second, alpha_next)
    shift = per_step * gain

    base = held_ref[:, :rows].T
    other = held_ref[:, rows : 2 * rows].T
    image = late_ref[:, :rows].T
    solution_ref[...] = full(base, alpha + gain) + full(other, gain_other)
    residual_ref[...] = full(base, first - shift) + full(other, second + shift) - full(image, gain_other)


def call(kernel, shapes, *args, scratch=(), dtypes=(jnp.float32, jnp.float32), limit=8):
    outs = pl.pallas_call(
        kernel,
        out_shape=tuple(jax.ShapeDtypeStruct(*shape) for shape in zip(shapes, dtypes)),
        in_specs=[pl.BlockSpec(memory_space=pltpu.VMEM if near else pl.ANY) for near, _ in map(place, args)],
        out_specs=tuple(pl.BlockSpec(memory_space=pltpu.VMEM) for _ in shapes),
        scratch_shapes=scratch,
        compiler_params=pltpu.CompilerParams(vmem_limit_bytes=limit * 2**20),
    )(*(value for _, value in map(place, args)))
    return outs if len(outs) > 1 else outs[0]


class Far:
    def __init__(self, value):
        self.value = value


def place(arg):
    if isinstance(arg, Far):
        return False, pltpu.with_memory_space_constraint(arg.value, pltpu.MemorySpace.HBM)
    return True, arg


def on_device(rows_n, cols_n, grads, seeds, bank, query_ids):
    rows, depth = grads.shape
    queries = query_ids.shape[0]
    mine = queries // cols_n
    lanes = 128
    pieces = (rows_n, mine, depth // rows_n)

    def reduce_row(part):
        total = call(sum_kernel, [part.shape], swap(part, "row"), dtypes=[part.dtype])
        return swap(total, "row")

    seeds = seeds.reshape(-1, lanes)
    picked, scale = call(
        functools.partial(pick_kernel, cols_n),
        [pieces, (1, rows)],
        Far(query_ids),
        Far(seeds),
        Far(bank),
        scratch=[
            pltpu.SMEM(query_ids.shape, jnp.int32),
            pltpu.VMEM(seeds.shape, jnp.int32),
            pltpu.VMEM(bank.shape, bank.dtype),
            pltpu.SemaphoreType.DMA((3,)),
        ],
        dtypes=[bank.dtype, jnp.float32],
    )
    chosen = reduce_row(picked)
    base, part, grads = call(
        base_kernel,
        [(mine, rows), pieces, grads.shape],
        chosen,
        scale,
        Far(grads),
        scratch=[pltpu.SemaphoreType.DMA((rows_n,))],
        dtypes=[jnp.float32, jnp.float32, grads.dtype],
    )
    back = reduce_row(part)
    wide = 2 * rows + lanes
    message, part = call(other_kernel, [(mine, wide), pieces], back, chosen, base, scale, grads)
    held = spread(message, "col", cols_n).reshape(queries, wide)
    back = reduce_row(part)
    image, moments = call(
        image_kernel, [(mine, rows), (mine, 4 * queries)], back, message, held, scale, grads
    )
    late = (cols_n, mine, rows + 4 * queries)
    late = swap(call(late_kernel, [late], spread(moments, "row", rows_n), image), "col")
    square = pltpu.VMEM((queries, queries), jnp.float32)
    return call(
        functools.partial(finish_kernel, rows),
        [(rows, queries), (rows, queries)],
        held,
        late.reshape(queries, rows + 4 * queries),
        scratch=[square, square],
    )


def solution(mesh):
    placed = (P("row", None), P(), P("row", None), P())

    def body(*args):
        return on_device(mesh.shape["row"], mesh.shape["col"], *args)

    return jax.shard_map(
        body,
        mesh=mesh,
        in_specs=placed,
        out_specs=(P("row", None), P("row", None)),
        check_vma=False,
    )
```

```python
import functools

import jax
import jax.numpy as jnp
from jax import lax
from jax.experimental import pallas as pl
from jax.experimental.pallas import tpu as pltpu
from jax.sharding import PartitionSpec as P

damping = 0.5


def full(left, right, dims=((1,), (0,))):
    return lax.dot_general(
        left,
        right,
        (dims, ((), ())),
        precision=lax.Precision.HIGHEST,
        preferred_element_type=jnp.float32,
    )


def two_terms(value):
    high = value.astype(jnp.bfloat16).astype(jnp.float32)
    return jnp.concatenate([high, value - high]).astype(jnp.bfloat16)


def both_terms(product):
    half = product.shape[0] // 2
    return product[:half] + product[half:]


def bf16_dot(left, right, right_dim):
    return lax.dot_general(
        left, right, (((1,), (right_dim,)), ((), ())), preferred_element_type=jnp.float32
    )


def halves(value):
    high = value.astype(jnp.bfloat16)
    return high, (value - high.astype(jnp.float32)).astype(jnp.bfloat16)


def product(left, right):
    high, low = halves(right)
    top = jnp.concatenate([high, low], axis=1)
    bottom = jnp.concatenate([high, jnp.zeros_like(low)], axis=1)
    both = jnp.dot(
        jnp.concatenate(halves(left), axis=1),
        jnp.concatenate([top, bottom], axis=0),
        preferred_element_type=jnp.float32,
    )
    columns = right.shape[1]
    return both[:, :columns] + both[:, columns:]


def swap(pieces, axis):
    return lax.all_to_all(pieces, axis, 0, 0, tiled=True)


def spread(piece, axis, size):
    return swap(jnp.broadcast_to(piece[None], (size,) + piece.shape), axis)


def inverse_spd(mat, eye, both_ref):
    size = mat.shape[0]
    on_diag = mat * eye
    across = lax.rsqrt(jnp.sum(on_diag, axis=0, keepdims=True))
    down = lax.rsqrt(jnp.sum(on_diag, axis=1, keepdims=True))
    unit = mat * across * down
    reach = jnp.sum(jnp.abs(unit), axis=1, keepdims=True)
    share = 1.0 / jnp.max(reach, axis=0, keepdims=True)
    left = eye - share * unit
    inv = share * (eye + left)
    left = product(left, left)

    def advance(inv, left):
        both = product(jnp.concatenate([inv, left]), left)
        return inv + both[:size], both[size:]

    for _ in range(4):
        inv, left = advance(inv, left)
    both_ref[:size] = inv
    both_ref[size:] = left

    def open_still(state):
        count, remainder = state
        return jnp.logical_and(count < 40, remainder > 1e-5)

    def again(state):
        inv, left = advance(both_ref[:size], both_ref[size:])
        both_ref[:size] = inv
        both_ref[size:] = left
        return state[0] + 1, jnp.sum(left * left)

    lax.while_loop(open_still, again, (0, jnp.sum(left * left)))
    inv = both_ref[:size]
    inv = inv + product(inv, both_ref[size:])
    return inv * across * down


def solve_with(mat, inv, right):
    first = product(inv, right)
    return first + product(inv, right - full(mat, first))


def pick_kernel(
    ids_hbm, seeds_hbm, bank_hbm, picked_ref, scale_ref, ids_ref, seeds_ref, bank_ref, sems
):
    copies = [
        pltpu.make_async_copy(source, target, sems.at[k])
        for k, (source, target) in enumerate(
            [(ids_hbm, ids_ref), (bank_hbm, bank_ref), (seeds_hbm, seeds_ref)]
        )
    ]
    for copy in copies:
        copy.start()
    parts, mine, width = picked_ref.shape
    bank_rows = bank_ref.shape[0]
    my_row = lax.axis_index("row")
    my_col = lax.axis_index("col")
    query = lax.broadcasted_iota(jnp.int32, (mine, bank_rows), 0)
    held = lax.broadcasted_iota(jnp.int32, (mine, bank_rows), 1)
    chosen = jnp.zeros((mine, bank_rows), jnp.bool_)
    copies[0].wait()
    for q in range(mine):
        local = ids_ref[my_col * mine + q] - my_row * bank_rows
        chosen = jnp.logical_or(chosen, jnp.logical_and(query == q, held == local))
    selector = jnp.where(chosen, 1.0, 0.0).astype(jnp.bfloat16)
    copies[1].wait()
    for k in range(parts):
        picked = bf16_dot(selector, bank_ref[:, k * width : (k + 1) * width], 0)
        picked_ref[k] = picked.astype(jnp.bfloat16)
    lanes = seeds_ref.shape[1]
    groups = scale_ref.shape[1] // lanes
    copies[2].wait()
    for k in range(groups):
        seeds = seeds_ref[pl.ds(my_row * groups + k, 1), :]
        scale_ref[:, k * lanes : (k + 1) * lanes] = jnp.exp2(seeds.astype(jnp.float32) / 4.0)


def sum_kernel(parts_ref, out_ref):
    total = parts_ref[0].astype(jnp.float32)
    for k in range(1, parts_ref.shape[0]):
        total += parts_ref[k].astype(jnp.float32)
    for k in range(out_ref.shape[0]):
        out_ref[k] = total.astype(out_ref.dtype)


def late_kernel(parts_ref, image_ref, out_ref):
    total = parts_ref[0]
    for k in range(1, parts_ref.shape[0]):
        total += parts_ref[k]
    late = jnp.concatenate([image_ref[...], total], axis=1)
    for k in range(out_ref.shape[0]):
        out_ref[k] = late


def partial_back(value, grads_ref, part_ref):
    terms = two_terms(value)
    parts, _, width = part_ref.shape
    for k in range(parts):
        product = bf16_dot(terms, grads_ref[:, k * width : (k + 1) * width], 0)
        part_ref[k] = both_terms(product)


def base_kernel(chosen_ref, scale_ref, grads_hbm, base_ref, part_ref, grads_ref, sems):
    parts, _, width = chosen_ref.shape
    copies = []
    for k in range(parts):
        block = (slice(None), pl.ds(k * width, width))
        copies.append(pltpu.make_async_copy(grads_hbm.at[block], grads_ref.at[block], sems.at[k]))
        copies[k].start()
    total = jnp.zeros(base_ref.shape, jnp.float32)
    for k in range(parts):
        copies[k].wait()
        total += bf16_dot(chosen_ref[k], grads_ref[:, k * width : (k + 1) * width], 1)
    scale = scale_ref[...]
    base = scale * total
    base_ref[...] = base
    partial_back(scale * base, grads_ref, part_ref)


def project(back_ref, grads_ref, width):
    parts, lead, _ = back_ref.shape
    total = jnp.zeros((2 * lead, grads_ref.shape[0]), jnp.float32)
    for k in range(parts):
        terms = two_terms(back_ref[k, :, :width])
        total += bf16_dot(terms, grads_ref[:, k * width : (k + 1) * width], 1)
    return both_terms(total)


def other_kernel(back_ref, chosen_ref, base_ref, scale_ref, grads_ref, message_ref, part_ref):
    parts, lead, width = back_ref.shape
    rows = base_ref.shape[1]
    square = jnp.zeros((lead, width), jnp.float32)
    curve = jnp.zeros((lead, width), jnp.float32)
    for k in range(parts):
        back = back_ref[k]
        square += chosen_ref[k].astype(jnp.float32) * back
        curve += back * back
    square = jnp.sum(square, axis=1, keepdims=True)
    curve = jnp.sum(curve, axis=1, keepdims=True)
    step = square / (curve + damping * square)
    base = base_ref[...]
    scale = scale_ref[...]
    other = base - step * (scale * project(back_ref, grads_ref, width) + damping * base)
    message_ref[:, :rows] = base
    message_ref[:, rows : 2 * rows] = other
    message_ref[:, 2 * rows :] = jnp.broadcast_to(step, (lead, message_ref.shape[1] - 2 * rows))
    partial_back(scale * other, grads_ref, part_ref)


def join_kernel(part_ref, held_ref, out_ref):
    parts, lead, width = part_ref.shape
    rows = (held_ref.shape[1] - 128) // 2
    base = held_ref[:, :rows]
    other = held_ref[:, rows : 2 * rows]
    last = ((1,), (1,))
    inner = [full(base, base, last), full(other, base, last), full(other, other, last)]
    for k in range(parts):
        out_ref[k, :, :width] = part_ref[k]
        for n, mat in enumerate(inner):
            lanes = slice(width + n * mat.shape[1], width + (n + 1) * mat.shape[1])
            out_ref[k, :, lanes] = mat[k * lead : (k + 1) * lead]


def image_kernel(back_ref, message_ref, held_ref, scale_ref, grads_ref, image_ref, inner_ref):
    rows = image_ref.shape[1]
    width = grads_ref.shape[1] // back_ref.shape[0]
    own_other = message_ref[:, rows : 2 * rows]
    image = scale_ref[...] * project(back_ref, grads_ref, width) + damping * own_other
    image_ref[...] = image
    inner_ref[...] = full(image, held_ref[:, rows : 2 * rows], ((1,), (1,)))


def first_kernel(width, back_ref, held_ref, solved_ref, terms_ref, both_ref):
    queries = held_ref.shape[0]
    rows = terms_ref.shape[0]
    parts = range(back_ref.shape[0])
    bb, tb, tt = (
        jnp.concatenate([back_ref[k, :, width + n * queries : width + (n + 1) * queries] for k in parts])
        for n in range(3)
    )
    per_step = 1.0 / held_ref[:, 2 * rows :]
    shape = (queries, queries)
    row_id = lax.broadcasted_iota(jnp.int32, shape, 0)
    eye = jnp.where(row_id == lax.broadcasted_iota(jnp.int32, shape, 1), 1.0, 0.0)

    bab = per_step * (bb - tb)
    bat = per_step * (tb.T - tt)
    tab = bat.T
    inv = inverse_spd(bab, eye, both_ref)
    alpha = solve_with(bab, inv, bb)
    second = per_step * alpha
    fresh = product(second.T, tb - full(tab, alpha))
    mixed = -solve_with(bab, inv, product(bat, second))
    for k, mat in enumerate([alpha, second, fresh, mixed, product(tab, mixed)]):
        solved_ref[k] = mat
    for k in range(2):
        block = held_ref[:, k * rows : (k + 1) * rows].T
        terms_ref[:, 2 * k * queries : 2 * (k + 1) * queries] = jnp.concatenate(halves(block), axis=1)


def finish_kernel(held_ref, solved_ref, terms_ref, late_ref, solution_ref, residual_ref, both_ref):
    queries = held_ref.shape[0]
    rows = terms_ref.shape[0]
    tat = late_ref[:, rows:]
    per_step = 1.0 / held_ref[:, 2 * rows :]
    alpha, second, fresh, mixed, lead = (solved_ref[k] for k in range(5))
    shape = (queries, queries)
    row_id = lax.broadcasted_iota(jnp.int32, shape, 0)
    eye = jnp.where(row_id == lax.broadcasted_iota(jnp.int32, shape, 1), 1.0, 0.0)
    curv = product(second.T, lead + product(tat, second))
    curv = 0.5 * (curv + curv.T)
    image = jnp.concatenate(halves(late_ref[:, :rows].T), axis=1)
    inv = inverse_spd(curv, eye, both_ref)
    alpha_next = solve_with(curv, inv, fresh)
    gain = product(jnp.concatenate([mixed, second]), alpha_next)
    gain, gain_other = gain[:queries], gain[queries:]
    shift = per_step * gain

    def times(terms, right):
        high, low = halves(right)
        both = jnp.dot(
            terms,
            jnp.concatenate(
                [
                    jnp.concatenate([high, low], axis=1),
                    jnp.concatenate([high, jnp.zeros_like(low)], axis=1),
                ]
            ),
            preferred_element_type=jnp.float32,
        )
        return both[:, : right.shape[1]] + both[:, right.shape[1] :]

    first = eye - second
    out = times(terms_ref[:, : 2 * queries], jnp.concatenate([alpha + gain, first - shift], axis=1))
    out += times(terms_ref[:, 2 * queries :], jnp.concatenate([gain_other, second + shift], axis=1))
    solution_ref[...] = out[:, :queries]
    residual_ref[...] = out[:, queries:] - times(image, gain_other)


def call(kernel, shapes, *args, scratch=(), dtypes=(jnp.float32, jnp.float32), limit=8):
    outs = pl.pallas_call(
        kernel,
        out_shape=tuple(jax.ShapeDtypeStruct(*shape) for shape in zip(shapes, dtypes)),
        in_specs=[pl.BlockSpec(memory_space=pltpu.VMEM if near else pl.ANY) for near, _ in map(place, args)],
        out_specs=tuple(pl.BlockSpec(memory_space=pltpu.VMEM) for _ in shapes),
        scratch_shapes=scratch,
        compiler_params=pltpu.CompilerParams(vmem_limit_bytes=limit * 2**20),
    )(*(value for _, value in map(place, args)))
    return outs if len(outs) > 1 else outs[0]


class Far:
    def __init__(self, value):
        self.value = value


def place(arg):
    if isinstance(arg, Far):
        return False, pltpu.with_memory_space_constraint(arg.value, pltpu.MemorySpace.HBM)
    return True, arg


def on_device(rows_n, cols_n, grads, seeds, bank, query_ids):
    rows, depth = grads.shape
    queries = query_ids.shape[0]
    mine = queries // cols_n
    lanes = 128
    pieces = (rows_n, mine, depth // rows_n)

    def reduce_row(part):
        total = call(sum_kernel, [part.shape], swap(part, "row"), dtypes=[part.dtype])
        return swap(total, "row")

    seeds = seeds.reshape(-1, lanes)
    picked, scale = call(
        pick_kernel,
        [pieces, (1, rows)],
        Far(query_ids),
        Far(seeds),
        Far(bank),
        scratch=[
            pltpu.SMEM(query_ids.shape, jnp.int32),
            pltpu.VMEM(seeds.shape, jnp.int32),
            pltpu.VMEM(bank.shape, bank.dtype),
            pltpu.SemaphoreType.DMA((3,)),
        ],
        dtypes=[bank.dtype, jnp.float32],
    )
    chosen = reduce_row(picked)
    base, part, grads = call(
        base_kernel,
        [(mine, rows), pieces, grads.shape],
        chosen,
        scale,
        Far(grads),
        scratch=[pltpu.SemaphoreType.DMA((rows_n,))],
        dtypes=[jnp.float32, jnp.float32, grads.dtype],
    )
    back = reduce_row(part)
    wide = 2 * rows + lanes
    message, part = call(other_kernel, [(mine, wide), pieces], back, chosen, base, scale, grads)
    held = spread(message, "col", cols_n).reshape(queries, wide)
    width = pieces[2]
    back = reduce_row(call(join_kernel, [(rows_n, mine, width + 3 * queries)], part, held))
    image, inner = call(
        image_kernel, [(mine, rows), (mine, queries)], back, message, held, scale, grads
    )
    both = pltpu.VMEM((2 * queries, queries), jnp.float32)
    solved, terms = call(
        functools.partial(first_kernel, width),
        [(5, queries, queries), (rows, 4 * queries)],
        back,
        held,
        scratch=[both],
        dtypes=[jnp.float32, jnp.bfloat16],
    )
    late = (cols_n, mine, rows + queries)
    inner = spread(inner, "row", rows_n)
    late = call(late_kernel, [late], inner, image)
    late = swap(late, "col")
    return call(
        finish_kernel,
        [(rows, queries), (rows, queries)],
        held,
        solved,
        terms,
        late.reshape(queries, rows + queries),
        scratch=[both],
    )


def solution(mesh):
    placed = (P("row", None), P(), P("row", None), P())

    def body(*args):
        return on_device(mesh.shape["row"], mesh.shape["col"], *args)

    return jax.shard_map(
        body,
        mesh=mesh,
        in_specs=placed,
        out_specs=(P("row", None), P("row", None)),
        check_vma=False,
    )
```

```python
import functools

import jax
import jax.numpy as jnp
from jax import lax
from jax.experimental import pallas as pl
from jax.experimental.pallas import tpu as pltpu
from jax.sharding import PartitionSpec as P


damping = 0.5


def full(left, right):
    return lax.dot_general(
        left,
        right,
        (((1,), (0,)), ((), ())),
        precision=lax.Precision.HIGHEST,
        preferred_element_type=jnp.float32,
    )


def two_terms(value):
    high = value.astype(jnp.bfloat16).astype(jnp.float32)
    return jnp.concatenate([high, value - high]).astype(jnp.bfloat16)


def both_terms(product):
    half = product.shape[0] // 2
    return product[:half] + product[half:]


def bf16_dot(left, right, right_dim):
    return lax.dot_general(
        left, right, (((1,), (right_dim,)), ((), ())), preferred_element_type=jnp.float32
    )


def halves(value):
    high = value.astype(jnp.bfloat16)
    return high, (value - high.astype(jnp.float32)).astype(jnp.bfloat16)


def product(left, right):
    high, low = halves(right)
    top = jnp.concatenate([high, low], axis=1)
    bottom = jnp.concatenate([high, jnp.zeros_like(low)], axis=1)
    both = jnp.dot(
        jnp.concatenate(halves(left), axis=1),
        jnp.concatenate([top, bottom], axis=0),
        preferred_element_type=jnp.float32,
    )
    columns = right.shape[1]
    return both[:, :columns] + both[:, columns:]


def row_product(left, right):
    high, low = halves(right)
    rows = right.shape[0]
    both = bf16_dot(
        jnp.concatenate(halves(left), axis=1),
        jnp.concatenate(
            [
                jnp.concatenate([high, high], axis=1),
                jnp.concatenate([low, jnp.zeros_like(low)], axis=1),
            ]
        ),
        1,
    )
    return both[:, :rows] + both[:, rows:]


def swap(pieces, axis):
    return lax.all_to_all(pieces, axis, 0, 0, tiled=True)


def spread(piece, axis, size):
    return swap(jnp.broadcast_to(piece[None], (size,) + piece.shape), axis)


def inverse_spd(mat, eye, both_ref):
    size = mat.shape[0]
    on_diag = mat * eye
    across = lax.rsqrt(jnp.sum(on_diag, axis=0, keepdims=True))
    down = lax.rsqrt(jnp.sum(on_diag, axis=1, keepdims=True))
    unit = mat * across * down
    reach = jnp.sum(jnp.abs(unit), axis=1, keepdims=True)
    share = 1.8 / jnp.max(reach, axis=0, keepdims=True)
    left = eye - share * unit
    inv = share * (eye + left)
    left = product(left, left)

    def advance(inv, left):
        both = product(jnp.concatenate([inv, left]), left)
        return inv + both[:size], both[size:]

    for _ in range(4):
        inv, left = advance(inv, left)
    both_ref[:size] = inv
    both_ref[size:] = left

    def open_still(state):
        count, remainder = state
        return jnp.logical_and(count < 40, remainder > 3e-4)

    def again(state):
        inv, left = advance(both_ref[:size], both_ref[size:])
        both_ref[:size] = inv
        both_ref[size:] = left
        return state[0] + 1, jnp.sum(left * left)

    lax.while_loop(open_still, again, (0, jnp.sum(left * left)))
    inv = both_ref[:size]
    inv = inv + product(inv, both_ref[size:])
    return inv * across * down


def solve_with(mat, inv, right):
    first = product(inv, right)
    return first + product(inv, right - full(mat, first))


def pick_kernel(
    ids_hbm, seeds_hbm, bank_hbm, picked_ref, scale_ref, ids_ref, seeds_ref, bank_ref, sems
):
    copies = [
        pltpu.make_async_copy(source, target, sems.at[k])
        for k, (source, target) in enumerate(
            [(ids_hbm, ids_ref), (bank_hbm, bank_ref), (seeds_hbm, seeds_ref)]
        )
    ]
    for copy in copies:
        copy.start()
    parts, mine, width = picked_ref.shape
    bank_rows = bank_ref.shape[0]
    my_row = lax.axis_index("row")
    my_col = lax.axis_index("col")
    query = lax.broadcasted_iota(jnp.int32, (mine, bank_rows), 0)
    held = lax.broadcasted_iota(jnp.int32, (mine, bank_rows), 1)
    chosen = jnp.zeros((mine, bank_rows), jnp.bool_)
    copies[0].wait()
    for q in range(mine):
        local = ids_ref[my_col * mine + q] - my_row * bank_rows
        chosen = jnp.logical_or(chosen, jnp.logical_and(query == q, held == local))
    selector = jnp.where(chosen, 1.0, 0.0).astype(jnp.bfloat16)
    copies[1].wait()
    for k in range(parts):
        picked = bf16_dot(selector, bank_ref[:, k * width : (k + 1) * width], 0)
        picked_ref[k] = picked.astype(jnp.bfloat16)
    lanes = seeds_ref.shape[1]
    groups = scale_ref.shape[1] // lanes
    copies[2].wait()
    for k in range(groups):
        seeds = seeds_ref[pl.ds(my_row * groups + k, 1), :]
        scale_ref[:, k * lanes : (k + 1) * lanes] = jnp.exp2(seeds.astype(jnp.float32) / 4.0)


def sum_kernel(parts_ref, out_ref):
    total = parts_ref[0].astype(jnp.float32)
    for k in range(1, parts_ref.shape[0]):
        total += parts_ref[k].astype(jnp.float32)
    for k in range(out_ref.shape[0]):
        out_ref[k] = total.astype(out_ref.dtype)


def late_kernel(parts_ref, image_ref, out_ref):
    total = parts_ref[0]
    for k in range(1, parts_ref.shape[0]):
        total += parts_ref[k]
    late = jnp.concatenate([image_ref[...], total], axis=1)
    for k in range(out_ref.shape[0]):
        out_ref[k] = late


def partial_back(value, grads_ref, part_ref):
    terms = two_terms(value)
    parts, _, width = part_ref.shape
    for k in range(parts):
        product = bf16_dot(terms, grads_ref[:, k * width : (k + 1) * width], 0)
        part_ref[k] = both_terms(product)


def base_kernel(chosen_ref, scale_ref, grads_hbm, base_ref, part_ref, grads_ref, sems):
    parts, _, width = chosen_ref.shape
    copies = []
    for k in range(parts):
        block = (slice(None), pl.ds(k * width, width))
        copies.append(pltpu.make_async_copy(grads_hbm.at[block], grads_ref.at[block], sems.at[k]))
        copies[k].start()
    total = jnp.zeros(base_ref.shape, jnp.float32)
    for k in range(parts):
        copies[k].wait()
        total += bf16_dot(chosen_ref[k], grads_ref[:, k * width : (k + 1) * width], 1)
    scale = scale_ref[...]
    base = scale * total
    base_ref[...] = base
    partial_back(scale * base, grads_ref, part_ref)


def project(back_ref, grads_ref, width):
    parts, lead, _ = back_ref.shape
    total = jnp.zeros((2 * lead, grads_ref.shape[0]), jnp.float32)
    for k in range(parts):
        terms = two_terms(back_ref[k, :, :width])
        total += bf16_dot(terms, grads_ref[:, k * width : (k + 1) * width], 1)
    return both_terms(total)


def other_kernel(back_ref, chosen_ref, base_ref, scale_ref, grads_ref, message_ref, part_ref):
    parts, lead, width = back_ref.shape
    rows = base_ref.shape[1]
    square = jnp.zeros((lead, width), jnp.float32)
    curve = jnp.zeros((lead, width), jnp.float32)
    for k in range(parts):
        back = back_ref[k]
        square += chosen_ref[k].astype(jnp.float32) * back
        curve += back * back
    square = jnp.sum(square, axis=1, keepdims=True)
    curve = jnp.sum(curve, axis=1, keepdims=True)
    step = square / (curve + damping * square)
    base = base_ref[...]
    scale = scale_ref[...]
    other = base - step * (scale * project(back_ref, grads_ref, width) + damping * base)
    message_ref[:, :rows] = base
    message_ref[:, rows : 2 * rows] = other
    message_ref[:, 2 * rows :] = jnp.broadcast_to(step, (lead, message_ref.shape[1] - 2 * rows))
    partial_back(scale * other, grads_ref, part_ref)


def join_kernel(part_ref, held_ref, out_ref):
    parts, lead, width = part_ref.shape
    rows = (held_ref.shape[1] - 128) // 2
    queries = held_ref.shape[0]
    stacked = jnp.concatenate([held_ref[:, :rows], held_ref[:, rows : 2 * rows]])
    square = row_product(stacked, stacked)
    inner = [square[:queries, :queries], square[queries:, :queries], square[queries:, queries:]]
    for k in range(parts):
        out_ref[k, :, :width] = part_ref[k]
        for n, mat in enumerate(inner):
            lanes = slice(width + n * mat.shape[1], width + (n + 1) * mat.shape[1])
            out_ref[k, :, lanes] = mat[k * lead : (k + 1) * lead]


def image_kernel(back_ref, message_ref, held_ref, scale_ref, grads_ref, image_ref, inner_ref):
    rows = image_ref.shape[1]
    width = grads_ref.shape[1] // back_ref.shape[0]
    own_other = message_ref[:, rows : 2 * rows]
    image = scale_ref[...] * project(back_ref, grads_ref, width) + damping * own_other
    image_ref[...] = image
    inner_ref[...] = row_product(image, held_ref[:, rows : 2 * rows])


def first_kernel(width, back_ref, held_ref, solved_ref, terms_ref, both_ref):
    queries = held_ref.shape[0]
    rows = terms_ref.shape[0]
    parts = range(back_ref.shape[0])
    bb, tb, tt = (
        jnp.concatenate([back_ref[k, :, width + n * queries : width + (n + 1) * queries] for k in parts])
        for n in range(3)
    )
    per_step = 1.0 / held_ref[:, 2 * rows :]
    shape = (queries, queries)
    row_id = lax.broadcasted_iota(jnp.int32, shape, 0)
    eye = jnp.where(row_id == lax.broadcasted_iota(jnp.int32, shape, 1), 1.0, 0.0)

    bab = per_step * (bb - tb)
    bat = per_step * (tb.T - tt)
    tab = bat.T
    inv = inverse_spd(bab, eye, both_ref)
    alpha = solve_with(bab, inv, bb)
    second = per_step * alpha
    fresh = product(second.T, tb - full(tab, alpha))
    mixed = -solve_with(bab, inv, product(bat, second))
    for k, mat in enumerate([alpha, second, fresh, mixed, product(tab, mixed)]):
        solved_ref[k] = mat
    for k in range(2):
        high, low = halves(held_ref[:, k * rows : (k + 1) * rows].T)
        for n, term in enumerate([high, low, high]):
            terms_ref[:, (3 * k + n) * queries : (3 * k + n + 1) * queries] = term


def finish_kernel(
    held_ref, solved_ref, terms_ref, late_ref, solution_hbm, residual_hbm, both_ref, out_ref, sems
):
    queries = held_ref.shape[0]
    rows = terms_ref.shape[0]
    tat = late_ref[:, rows:]
    per_step = 1.0 / held_ref[:, 2 * rows :]
    alpha, second, fresh, mixed, lead = (solved_ref[k] for k in range(5))
    shape = (queries, queries)
    row_id = lax.broadcasted_iota(jnp.int32, shape, 0)
    eye = jnp.where(row_id == lax.broadcasted_iota(jnp.int32, shape, 1), 1.0, 0.0)
    curv = product(second.T, lead + product(tat, second))
    curv = 0.5 * (curv + curv.T)
    high, low = halves(late_ref[:, :rows].T)
    image = jnp.concatenate([high, low, high], axis=1)
    inv = inverse_spd(curv, eye, both_ref)
    alpha_next = solve_with(curv, inv, fresh)
    gain = product(jnp.concatenate([mixed, second]), alpha_next)
    gain, gain_other = gain[:queries], gain[queries:]
    shift = per_step * gain
    weights = []
    for pair in (
        (alpha + gain, eye - second - shift),
        (gain_other, second + shift),
        (jnp.zeros(shape, jnp.float32), -gain_other),
    ):
        high, low = halves(jnp.concatenate(pair, axis=1))
        weights += [high, high, low]
    weights = jnp.concatenate(weights)
    copies = []
    step = rows // 2
    for k in range(2):
        block = pl.ds(k * step, step)
        terms = jnp.concatenate([terms_ref[block], image[k * step : (k + 1) * step]], axis=1)
        out_ref[block] = jnp.dot(terms, weights, preferred_element_type=jnp.float32)
        for n, target in enumerate([solution_hbm, residual_hbm]):
            source = out_ref.at[block, pl.ds(n * queries, queries)]
            copies.append(pltpu.make_async_copy(source, target.at[block], sems.at[2 * k + n]))
            copies[-1].start()
    for copy in copies:
        copy.wait()


def call(kernel, shapes, *args, scratch=(), dtypes=(jnp.float32, jnp.float32), out_space=pltpu.VMEM):
    outs = pl.pallas_call(
        kernel,
        out_shape=tuple(jax.ShapeDtypeStruct(*shape) for shape in zip(shapes, dtypes)),
        in_specs=[pl.BlockSpec(memory_space=pltpu.VMEM if near else pl.ANY) for near, _ in map(place, args)],
        out_specs=tuple(pl.BlockSpec(memory_space=out_space) for _ in shapes),
        scratch_shapes=scratch,
        compiler_params=pltpu.CompilerParams(vmem_limit_bytes=2**23),
    )(*(value for _, value in map(place, args)))
    return outs if len(outs) > 1 else outs[0]


class Far:
    def __init__(self, value):
        self.value = value


def place(arg):
    if isinstance(arg, Far):
        return False, pltpu.with_memory_space_constraint(arg.value, pltpu.MemorySpace.HBM)
    return True, arg


def on_device(rows_n, cols_n, grads, seeds, bank, query_ids):
    rows, depth = grads.shape
    queries = query_ids.shape[0]
    mine = queries // cols_n
    lanes = 128
    pieces = (rows_n, mine, depth // rows_n)

    def reduce_row(part):
        total = call(sum_kernel, [part.shape], swap(part, "row"), dtypes=[part.dtype])
        return swap(total, "row")

    seeds = seeds.reshape(-1, lanes)
    picked, scale = call(
        pick_kernel,
        [pieces, (1, rows)],
        Far(query_ids),
        Far(seeds),
        Far(bank),
        scratch=[
            pltpu.SMEM(query_ids.shape, jnp.int32),
            pltpu.VMEM(seeds.shape, jnp.int32),
            pltpu.VMEM(bank.shape, bank.dtype),
            pltpu.SemaphoreType.DMA((3,)),
        ],
        dtypes=[bank.dtype, jnp.float32],
    )
    chosen = reduce_row(picked)
    base, part, grads = call(
        base_kernel,
        [(mine, rows), pieces, grads.shape],
        chosen,
        scale,
        Far(grads),
        scratch=[pltpu.SemaphoreType.DMA((rows_n,))],
        dtypes=[jnp.float32, jnp.float32, grads.dtype],
    )
    back = reduce_row(part)
    wide = 2 * rows + lanes
    message, part = call(other_kernel, [(mine, wide), pieces], back, chosen, base, scale, grads)
    held = spread(message, "col", cols_n).reshape(queries, wide)
    width = pieces[2]
    back = reduce_row(call(join_kernel, [(rows_n, mine, width + 3 * queries)], part, held))
    image, inner = call(
        image_kernel, [(mine, rows), (mine, queries)], back, message, held, scale, grads
    )
    both = pltpu.VMEM((2 * queries, queries), jnp.float32)
    solved, terms = call(
        functools.partial(first_kernel, width),
        [(5, queries, queries), (rows, 6 * queries)],
        back,
        held,
        scratch=[both],
        dtypes=[jnp.float32, jnp.bfloat16],
    )
    late = (cols_n, mine, rows + queries)
    inner = spread(inner, "row", rows_n)
    late = call(late_kernel, [late], inner, image)
    late = swap(late, "col")
    return call(
        finish_kernel,
        [(rows, queries), (rows, queries)],
        held,
        solved,
        terms,
        late.reshape(queries, rows + queries),
        scratch=[both, pltpu.VMEM((rows, 2 * queries), jnp.float32), pltpu.SemaphoreType.DMA((4,))],
        out_space=pl.ANY,
    )


def solution(mesh):
    placed = (P("row", None), P(), P("row", None), P())

    def body(*args):
        return on_device(mesh.shape["row"], mesh.shape["col"], *args)

    return jax.shard_map(
        body,
        mesh=mesh,
        in_specs=placed,
        out_specs=(P("row", None), P("row", None)),
        check_vma=False,
    )
```

```python
import functools

import jax
import jax.numpy as jnp
from jax import lax
from jax.experimental import pallas as pl
from jax.experimental.pallas import tpu as pltpu
from jax.sharding import PartitionSpec as P


damping = 0.5


def full(left, right):
    return lax.dot_general(
        left,
        right,
        (((1,), (0,)), ((), ())),
        precision=lax.Precision.HIGHEST,
        preferred_element_type=jnp.float32,
    )


def two_terms(value):
    high = value.astype(jnp.bfloat16).astype(jnp.float32)
    return jnp.concatenate([high, value - high]).astype(jnp.bfloat16)


def both_terms(product):
    half = product.shape[0] // 2
    return product[:half] + product[half:]


def bf16_dot(left, right, right_dim):
    return lax.dot_general(
        left, right, (((1,), (right_dim,)), ((), ())), preferred_element_type=jnp.float32
    )


def halves(value):
    high = value.astype(jnp.bfloat16)
    return high, (value - high.astype(jnp.float32)).astype(jnp.bfloat16)


def product(left, right):
    high, low = halves(right)
    top = jnp.concatenate([high, low], axis=1)
    bottom = jnp.concatenate([high, jnp.zeros_like(low)], axis=1)
    both = jnp.dot(
        jnp.concatenate(halves(left), axis=1),
        jnp.concatenate([top, bottom], axis=0),
        preferred_element_type=jnp.float32,
    )
    columns = right.shape[1]
    return both[:, :columns] + both[:, columns:]


def row_product(left, right):
    high, low = halves(right)
    rows = right.shape[0]
    both = bf16_dot(
        jnp.concatenate(halves(left), axis=1),
        jnp.concatenate(
            [
                jnp.concatenate([high, high], axis=1),
                jnp.concatenate([low, jnp.zeros_like(low)], axis=1),
            ]
        ),
        1,
    )
    return both[:, :rows] + both[:, rows:]


def swap(pieces, axis):
    return lax.all_to_all(pieces, axis, 0, 0, tiled=True)


def spread(piece, axis, size):
    return swap(jnp.broadcast_to(piece[None], (size,) + piece.shape), axis)


def inverse_spd(mat, eye, both_ref):
    size = mat.shape[0]
    on_diag = mat * eye
    across = lax.rsqrt(jnp.sum(on_diag, axis=0, keepdims=True))
    down = lax.rsqrt(jnp.sum(on_diag, axis=1, keepdims=True))
    unit = mat * across * down
    reach = jnp.sum(jnp.abs(unit), axis=1, keepdims=True)
    share = 1.8 / jnp.max(reach, axis=0, keepdims=True)
    left = eye - share * unit
    inv = share * (eye + left)
    left = product(left, left)

    def advance(inv, left):
        both = product(jnp.concatenate([inv, left]), left)
        return inv + both[:size], both[size:]

    for _ in range(4):
        inv, left = advance(inv, left)
    both_ref[:size] = inv
    both_ref[size:] = left

    def open_still(state):
        count, remainder = state
        return jnp.logical_and(count < 40, remainder > 3e-4)

    def again(state):
        inv, left = advance(both_ref[:size], both_ref[size:])
        both_ref[:size] = inv
        both_ref[size:] = left
        return state[0] + 1, jnp.sum(left * left)

    lax.while_loop(open_still, again, (0, jnp.sum(left * left)))
    inv = both_ref[:size]
    inv = inv + product(inv, both_ref[size:])
    return inv * across * down


def solve_with(mat, inv, right):
    first = product(inv, right)
    return first + product(inv, right - full(mat, first))


def pick_kernel(
    ids_hbm, seeds_hbm, bank_hbm, picked_ref, scale_ref, ids_ref, seeds_ref, bank_ref, sems
):
    copies = [
        pltpu.make_async_copy(source, target, sems.at[k])
        for k, (source, target) in enumerate(
            [(ids_hbm, ids_ref), (bank_hbm, bank_ref), (seeds_hbm, seeds_ref)]
        )
    ]
    for copy in copies:
        copy.start()
    parts, mine, width = picked_ref.shape
    bank_rows = bank_ref.shape[0]
    my_row = lax.axis_index("row")
    my_col = lax.axis_index("col")
    query = lax.broadcasted_iota(jnp.int32, (mine, bank_rows), 0)
    held = lax.broadcasted_iota(jnp.int32, (mine, bank_rows), 1)
    chosen = jnp.zeros((mine, bank_rows), jnp.bool_)
    copies[0].wait()
    for q in range(mine):
        local = ids_ref[my_col * mine + q] - my_row * bank_rows
        chosen = jnp.logical_or(chosen, jnp.logical_and(query == q, held == local))
    selector = jnp.where(chosen, 1.0, 0.0).astype(jnp.bfloat16)
    copies[1].wait()
    for k in range(parts):
        picked = bf16_dot(selector, bank_ref[:, k * width : (k + 1) * width], 0)
        picked_ref[k] = picked.astype(jnp.bfloat16)
    lanes = seeds_ref.shape[1]
    groups = scale_ref.shape[1] // lanes
    copies[2].wait()
    for k in range(groups):
        seeds = seeds_ref[pl.ds(my_row * groups + k, 1), :]
        scale_ref[:, k * lanes : (k + 1) * lanes] = jnp.exp2(seeds.astype(jnp.float32) / 4.0)


def sum_kernel(parts_ref, out_ref):
    total = parts_ref[0].astype(jnp.float32)
    for k in range(1, parts_ref.shape[0]):
        total += parts_ref[k].astype(jnp.float32)
    for k in range(out_ref.shape[0]):
        out_ref[k] = total.astype(out_ref.dtype)


def late_kernel(parts_ref, image_ref, out_ref):
    total = parts_ref[0]
    for k in range(1, parts_ref.shape[0]):
        total += parts_ref[k]
    late = jnp.concatenate([image_ref[...], total], axis=1)
    for k in range(out_ref.shape[0]):
        out_ref[k] = late


def partial_back(value, grads_ref, part_ref):
    terms = two_terms(value)
    parts, _, width = part_ref.shape
    for k in range(parts):
        product = bf16_dot(terms, grads_ref[:, k * width : (k + 1) * width], 0)
        part_ref[k] = both_terms(product)


def base_kernel(
    chosen_ref, scale_ref, grads_hbm, base_ref, part_ref, grads_ref, turned_ref, sems
):
    parts, _, width = chosen_ref.shape
    copies = []
    for k in range(parts):
        block = (slice(None), pl.ds(k * width, width))
        copies.append(pltpu.make_async_copy(grads_hbm.at[block], grads_ref.at[block], sems.at[k]))
        copies[k].start()
    total = jnp.zeros(base_ref.shape, jnp.float32)
    for k in range(parts):
        copies[k].wait()
        turned = grads_ref[:, k * width : (k + 1) * width].T
        turned_ref[k * width : (k + 1) * width] = turned
        total += bf16_dot(chosen_ref[k], turned, 0)
    scale = scale_ref[...]
    base = scale * total
    base_ref[...] = base
    partial_back(scale * base, grads_ref, part_ref)


def project(back_ref, turned_ref, width):
    parts, lead, _ = back_ref.shape
    total = jnp.zeros((2 * lead, turned_ref.shape[1]), jnp.float32)
    for k in range(parts):
        terms = two_terms(back_ref[k, :, :width])
        total += bf16_dot(terms, turned_ref[k * width : (k + 1) * width], 0)
    return both_terms(total)


def other_kernel(
    back_ref, chosen_ref, base_ref, scale_ref, grads_ref, turned_ref, message_ref, part_ref
):
    parts, lead, width = back_ref.shape
    rows = base_ref.shape[1]
    square = jnp.zeros((lead, width), jnp.float32)
    curve = jnp.zeros((lead, width), jnp.float32)
    for k in range(parts):
        back = back_ref[k]
        square += chosen_ref[k].astype(jnp.float32) * back
        curve += back * back
    square = jnp.sum(square, axis=1, keepdims=True)
    curve = jnp.sum(curve, axis=1, keepdims=True)
    step = square / (curve + damping * square)
    base = base_ref[...]
    scale = scale_ref[...]
    other = base - step * (scale * project(back_ref, turned_ref, width) + damping * base)
    message_ref[:, :rows] = base
    message_ref[:, rows : 2 * rows] = other
    message_ref[:, 2 * rows :] = jnp.broadcast_to(step, (lead, message_ref.shape[1] - 2 * rows))
    partial_back(scale * other, grads_ref, part_ref)


def join_kernel(part_ref, held_ref, out_ref):
    parts, lead, width = part_ref.shape
    rows = (held_ref.shape[1] - 128) // 2
    queries = held_ref.shape[0]
    stacked = jnp.concatenate([held_ref[:, :rows], held_ref[:, rows : 2 * rows]])
    square = row_product(stacked, stacked)
    inner = [square[:queries, :queries], square[queries:, :queries], square[queries:, queries:]]
    for k in range(parts):
        out_ref[k, :, :width] = part_ref[k]
        for n, mat in enumerate(inner):
            lanes = slice(width + n * mat.shape[1], width + (n + 1) * mat.shape[1])
            out_ref[k, :, lanes] = mat[k * lead : (k + 1) * lead]


def image_kernel(back_ref, message_ref, held_ref, scale_ref, turned_ref, image_ref, inner_ref):
    rows = image_ref.shape[1]
    width = turned_ref.shape[0] // back_ref.shape[0]
    own_other = message_ref[:, rows : 2 * rows]
    image = scale_ref[...] * project(back_ref, turned_ref, width) + damping * own_other
    image_ref[...] = image
    inner_ref[...] = row_product(image, held_ref[:, rows : 2 * rows])


def first_kernel(width, back_ref, held_ref, solved_ref, terms_ref, both_ref):
    queries = held_ref.shape[0]
    rows = terms_ref.shape[0]
    parts = range(back_ref.shape[0])
    bb, tb, tt = (
        jnp.concatenate([back_ref[k, :, width + n * queries : width + (n + 1) * queries] for k in parts])
        for n in range(3)
    )
    per_step = 1.0 / held_ref[:, 2 * rows :]
    shape = (queries, queries)
    row_id = lax.broadcasted_iota(jnp.int32, shape, 0)
    eye = jnp.where(row_id == lax.broadcasted_iota(jnp.int32, shape, 1), 1.0, 0.0)

    bab = per_step * (bb - tb)
    bat = per_step * (tb.T - tt)
    tab = bat.T
    inv = inverse_spd(bab, eye, both_ref)
    alpha = solve_with(bab, inv, bb)
    second = per_step * alpha
    fresh = product(second.T, tb - full(tab, alpha))
    mixed = -solve_with(bab, inv, product(bat, second))
    for k, mat in enumerate([alpha, second, fresh, mixed, product(tab, mixed)]):
        solved_ref[k] = mat
    for k in range(2):
        high, low = halves(held_ref[:, k * rows : (k + 1) * rows].T)
        for n, term in enumerate([high, low, high]):
            terms_ref[:, (3 * k + n) * queries : (3 * k + n + 1) * queries] = term


def finish_kernel(
    held_ref, solved_ref, terms_ref, late_ref, solution_hbm, residual_hbm, both_ref, out_ref, sems
):
    queries = held_ref.shape[0]
    rows = terms_ref.shape[0]
    tat = late_ref[:, rows:]
    per_step = 1.0 / held_ref[:, 2 * rows :]
    alpha, second, fresh, mixed, lead = (solved_ref[k] for k in range(5))
    shape = (queries, queries)
    row_id = lax.broadcasted_iota(jnp.int32, shape, 0)
    eye = jnp.where(row_id == lax.broadcasted_iota(jnp.int32, shape, 1), 1.0, 0.0)
    curv = product(second.T, lead + product(tat, second))
    curv = 0.5 * (curv + curv.T)
    high, low = halves(late_ref[:, :rows].T)
    image = jnp.concatenate([high, low, high], axis=1)
    inv = inverse_spd(curv, eye, both_ref)
    alpha_next = solve_with(curv, inv, fresh)
    gain = product(jnp.concatenate([mixed, second]), alpha_next)
    gain, gain_other = gain[:queries], gain[queries:]
    shift = per_step * gain
    weights = []
    for pair in (
        (alpha + gain, eye - second - shift),
        (gain_other, second + shift),
        (jnp.zeros(shape, jnp.float32), -gain_other),
    ):
        high, low = halves(jnp.concatenate(pair, axis=1))
        weights += [high, high, low]
    weights = jnp.concatenate(weights)
    copies = []
    step = rows // 2
    for k in range(2):
        block = pl.ds(k * step, step)
        terms = jnp.concatenate([terms_ref[block], image[k * step : (k + 1) * step]], axis=1)
        out_ref[block] = jnp.dot(terms, weights, preferred_element_type=jnp.float32)
        for n, target in enumerate([solution_hbm, residual_hbm]):
            source = out_ref.at[block, pl.ds(n * queries, queries)]
            copies.append(pltpu.make_async_copy(source, target.at[block], sems.at[2 * k + n]))
            copies[-1].start()
    for copy in copies:
        copy.wait()


def call(kernel, shapes, *args, scratch=(), dtypes=(jnp.float32, jnp.float32), out_space=pltpu.VMEM):
    outs = pl.pallas_call(
        kernel,
        out_shape=tuple(jax.ShapeDtypeStruct(*shape) for shape in zip(shapes, dtypes)),
        in_specs=[pl.BlockSpec(memory_space=pltpu.VMEM if near else pl.ANY) for near, _ in map(place, args)],
        out_specs=tuple(pl.BlockSpec(memory_space=out_space) for _ in shapes),
        scratch_shapes=scratch,
        compiler_params=pltpu.CompilerParams(vmem_limit_bytes=2**23),
    )(*(value for _, value in map(place, args)))
    return outs if len(outs) > 1 else outs[0]


class Far:
    def __init__(self, value):
        self.value = value


def place(arg):
    if isinstance(arg, Far):
        return False, pltpu.with_memory_space_constraint(arg.value, pltpu.MemorySpace.HBM)
    return True, arg


def on_device(rows_n, cols_n, grads, seeds, bank, query_ids):
    rows, depth = grads.shape
    queries = query_ids.shape[0]
    mine = queries // cols_n
    lanes = 128
    pieces = (rows_n, mine, depth // rows_n)

    def reduce_row(part):
        total = call(sum_kernel, [part.shape], swap(part, "row"), dtypes=[part.dtype])
        return swap(total, "row")

    seeds = seeds.reshape(-1, lanes)
    picked, scale = call(
        pick_kernel,
        [pieces, (1, rows)],
        Far(query_ids),
        Far(seeds),
        Far(bank),
        scratch=[
            pltpu.SMEM(query_ids.shape, jnp.int32),
            pltpu.VMEM(seeds.shape, jnp.int32),
            pltpu.VMEM(bank.shape, bank.dtype),
            pltpu.SemaphoreType.DMA((3,)),
        ],
        dtypes=[bank.dtype, jnp.float32],
    )
    chosen = reduce_row(picked)
    base, part, grads, turned = call(
        base_kernel,
        [(mine, rows), pieces, grads.shape, (depth, rows)],
        chosen,
        scale,
        Far(grads),
        scratch=[pltpu.SemaphoreType.DMA((rows_n,))],
        dtypes=[jnp.float32, jnp.float32, grads.dtype, grads.dtype],
    )
    back = reduce_row(part)
    wide = 2 * rows + lanes
    message, part = call(other_kernel, [(mine, wide), pieces], back, chosen, base, scale, grads, turned)
    held = spread(message, "col", cols_n).reshape(queries, wide)
    width = pieces[2]
    back = reduce_row(call(join_kernel, [(rows_n, mine, width + 3 * queries)], part, held))
    image, inner = call(
        image_kernel, [(mine, rows), (mine, queries)], back, message, held, scale, turned
    )
    both = pltpu.VMEM((2 * queries, queries), jnp.float32)
    solved, terms = call(
        functools.partial(first_kernel, width),
        [(5, queries, queries), (rows, 6 * queries)],
        back,
        held,
        scratch=[both],
        dtypes=[jnp.float32, jnp.bfloat16],
    )
    late = (cols_n, mine, rows + queries)
    inner = spread(inner, "row", rows_n)
    late = call(late_kernel, [late], inner, image)
    late = swap(late, "col")
    return call(
        finish_kernel,
        [(rows, queries), (rows, queries)],
        held,
        solved,
        terms,
        late.reshape(queries, rows + queries),
        scratch=[both, pltpu.VMEM((rows, 2 * queries), jnp.float32), pltpu.SemaphoreType.DMA((4,))],
        out_space=pl.ANY,
    )


def solution(mesh):
    placed = (P("row", None), P(), P("row", None), P())

    def body(*args):
        return on_device(mesh.shape["row"], mesh.shape["col"], *args)

    return jax.shard_map(
        body,
        mesh=mesh,
        in_specs=placed,
        out_specs=(P("row", None), P("row", None)),
        check_vma=False,
    )
```

```python
import functools

import jax
import jax.numpy as jnp
from jax import lax
from jax.experimental import pallas as pl
from jax.experimental.pallas import tpu as pltpu
from jax.sharding import PartitionSpec as P


damping = 0.5


def full(left, right):
    return lax.dot_general(
        left,
        right,
        (((1,), (0,)), ((), ())),
        precision=lax.Precision.HIGHEST,
        preferred_element_type=jnp.float32,
    )


def two_terms(value):
    high = value.astype(jnp.bfloat16).astype(jnp.float32)
    return jnp.concatenate([high, value - high]).astype(jnp.bfloat16)


def both_terms(product):
    half = product.shape[0] // 2
    return product[:half] + product[half:]


def bf16_dot(left, right, right_dim):
    return lax.dot_general(
        left, right, (((1,), (right_dim,)), ((), ())), preferred_element_type=jnp.float32
    )


def halves(value):
    high = value.astype(jnp.bfloat16)
    return high, (value - high.astype(jnp.float32)).astype(jnp.bfloat16)


def product(left, right):
    high, low = halves(right)
    top = jnp.concatenate([high, low], axis=1)
    bottom = jnp.concatenate([high, jnp.zeros_like(low)], axis=1)
    both = jnp.dot(
        jnp.concatenate(halves(left), axis=1),
        jnp.concatenate([top, bottom], axis=0),
        preferred_element_type=jnp.float32,
    )
    columns = right.shape[1]
    return both[:, :columns] + both[:, columns:]


def row_product(left, right):
    high, low = halves(right)
    rows = right.shape[0]
    both = bf16_dot(
        jnp.concatenate(halves(left), axis=1),
        jnp.concatenate(
            [
                jnp.concatenate([high, high], axis=1),
                jnp.concatenate([low, jnp.zeros_like(low)], axis=1),
            ]
        ),
        1,
    )
    return both[:, :rows] + both[:, rows:]


def swap(pieces, axis):
    return lax.all_to_all(pieces, axis, 0, 0, tiled=True)


def spread(piece, axis, size):
    return swap(jnp.broadcast_to(piece[None], (size,) + piece.shape), axis)


def inverse_spd(mat, eye, both_ref):
    size = mat.shape[0]
    on_diag = mat * eye
    across = lax.rsqrt(jnp.sum(on_diag, axis=0, keepdims=True))
    down = lax.rsqrt(jnp.sum(on_diag, axis=1, keepdims=True))
    unit = mat * across * down
    reach = jnp.sum(jnp.abs(unit), axis=1, keepdims=True)
    share = 1.8 / jnp.max(reach, axis=0, keepdims=True)
    left = eye - share * unit
    inv = share * (eye + left)
    left = product(left, left)

    def advance(inv, left):
        both = product(jnp.concatenate([inv, left]), left)
        return inv + both[:size], both[size:]

    for _ in range(4):
        inv, left = advance(inv, left)
    both_ref[:size] = inv
    both_ref[size:] = left

    def open_still(state):
        count, remainder = state
        return jnp.logical_and(count < 40, remainder > 3e-4)

    def again(state):
        inv, left = advance(both_ref[:size], both_ref[size:])
        both_ref[:size] = inv
        both_ref[size:] = left
        return state[0] + 1, jnp.sum(left * left)

    lax.while_loop(open_still, again, (0, jnp.sum(left * left)))
    inv = both_ref[:size]
    inv = inv + product(inv, both_ref[size:])
    return inv * across * down


def solve_with(mat, inv, right):
    first = product(inv, right)
    return first + product(inv, right - full(mat, first))


def pick_kernel(
    ids_hbm, seeds_hbm, bank_hbm, picked_ref, scale_ref, ids_ref, seeds_ref, bank_ref, sems
):
    copies = [
        pltpu.make_async_copy(source, target, sems.at[k])
        for k, (source, target) in enumerate(
            [(ids_hbm, ids_ref), (bank_hbm, bank_ref), (seeds_hbm, seeds_ref)]
        )
    ]
    for copy in copies:
        copy.start()
    parts, mine, width = picked_ref.shape
    bank_rows = bank_ref.shape[0]
    my_row = lax.axis_index("row")
    my_col = lax.axis_index("col")
    query = lax.broadcasted_iota(jnp.int32, (mine, bank_rows), 0)
    held = lax.broadcasted_iota(jnp.int32, (mine, bank_rows), 1)
    chosen = jnp.zeros((mine, bank_rows), jnp.bool_)
    copies[0].wait()
    for q in range(mine):
        local = ids_ref[my_col * mine + q] - my_row * bank_rows
        chosen = jnp.logical_or(chosen, jnp.logical_and(query == q, held == local))
    selector = jnp.where(chosen, 1.0, 0.0).astype(jnp.bfloat16)
    copies[1].wait()
    for k in range(parts):
        picked = bf16_dot(selector, bank_ref[:, k * width : (k + 1) * width], 0)
        picked_ref[k] = picked.astype(jnp.bfloat16)
    lanes = seeds_ref.shape[1]
    groups = scale_ref.shape[1] // lanes
    copies[2].wait()
    for k in range(groups):
        seeds = seeds_ref[pl.ds(my_row * groups + k, 1), :]
        scale_ref[:, k * lanes : (k + 1) * lanes] = jnp.exp2(seeds.astype(jnp.float32) / 4.0)


def sum_kernel(parts_ref, out_ref):
    total = parts_ref[0].astype(jnp.float32)
    for k in range(1, parts_ref.shape[0]):
        total += parts_ref[k].astype(jnp.float32)
    for k in range(out_ref.shape[0]):
        out_ref[k] = total.astype(out_ref.dtype)


def late_kernel(parts_ref, image_ref, out_ref):
    total = parts_ref[0]
    for k in range(1, parts_ref.shape[0]):
        total += parts_ref[k]
    late = jnp.concatenate([image_ref[...], total], axis=1)
    for k in range(out_ref.shape[0]):
        out_ref[k] = late


def partial_back(value, grads_ref, part_ref):
    terms = two_terms(value)
    parts, _, width = part_ref.shape
    for k in range(parts):
        product = bf16_dot(terms, grads_ref[:, k * width : (k + 1) * width], 0)
        part_ref[k] = both_terms(product)


def base_kernel(
    chosen_ref, scale_ref, grads_hbm, base_ref, part_ref, grads_ref, turned_ref, sems
):
    parts, _, width = chosen_ref.shape
    copies = []
    for k in range(parts):
        block = (slice(None), pl.ds(k * width, width))
        copies.append(pltpu.make_async_copy(grads_hbm.at[block], grads_ref.at[block], sems.at[k]))
        copies[k].start()
    total = jnp.zeros(base_ref.shape, jnp.float32)
    for k in range(parts):
        copies[k].wait()
        turned = grads_ref[:, k * width : (k + 1) * width].T
        turned_ref[k * width : (k + 1) * width] = turned
        total += bf16_dot(chosen_ref[k], turned, 0)
    scale = scale_ref[...]
    base = scale * total
    base_ref[...] = base
    partial_back(scale * base, grads_ref, part_ref)


def project(back_ref, turned_ref, width):
    parts, lead, _ = back_ref.shape
    total = jnp.zeros((2 * lead, turned_ref.shape[1]), jnp.float32)
    for k in range(parts):
        terms = two_terms(back_ref[k, :, :width])
        total += bf16_dot(terms, turned_ref[k * width : (k + 1) * width], 0)
    return both_terms(total)


def other_kernel(
    back_ref, chosen_ref, base_ref, scale_ref, grads_ref, turned_ref, message_ref, part_ref
):
    parts, lead, width = back_ref.shape
    rows = base_ref.shape[1]
    square = jnp.zeros((lead, width), jnp.float32)
    curve = jnp.zeros((lead, width), jnp.float32)
    for k in range(parts):
        back = back_ref[k]
        square += chosen_ref[k].astype(jnp.float32) * back
        curve += back * back
    square = jnp.sum(square, axis=1, keepdims=True)
    curve = jnp.sum(curve, axis=1, keepdims=True)
    step = square / (curve + damping * square)
    base = base_ref[...]
    scale = scale_ref[...]
    other = base - step * (scale * project(back_ref, turned_ref, width) + damping * base)
    message_ref[:, :rows] = base
    message_ref[:, rows : 2 * rows] = other
    message_ref[:, 2 * rows :] = jnp.broadcast_to(step, (lead, message_ref.shape[1] - 2 * rows))
    partial_back(scale * other, grads_ref, part_ref)


def masks(size):
    row = lax.broadcasted_iota(jnp.int32, (size, size), 0)
    column = lax.broadcasted_iota(jnp.int32, (size, size), 1)
    after = jnp.logical_or(column == row + 1, row == column + size - 1)
    return column <= row, after, column == row + size - 1, column == row


def join_kernel(part_ref, held_ref, out_ref):
    parts, lead, width = part_ref.shape
    rows = (held_ref.shape[1] - 128) // 2
    queries = held_ref.shape[0]
    stacked = jnp.concatenate([held_ref[:, :rows], held_ref[:, rows : 2 * rows]])
    square = row_product(stacked, stacked)
    bb, tb, tt = square[:queries, :queries], square[queries:, :queries], square[queries:, queries:]
    lower, after, corner, eye = masks(queries)
    bab = 1.0 / held_ref[:, 2 * rows :] * (bb - tb)
    on_diag = jnp.sum(jnp.where(eye, tt, 0.0), axis=1, keepdims=True)
    inner = [
        jnp.where(lower, bb, tt),
        jnp.where(after, on_diag, jnp.where(jnp.logical_or(lower, corner), bab, 0.0)),
    ]
    for k in range(parts):
        out_ref[k, :, :width] = part_ref[k]
        for n, mat in enumerate(inner):
            lanes = slice(width + n * mat.shape[1], width + (n + 1) * mat.shape[1])
            out_ref[k, :, lanes] = mat[k * lead : (k + 1) * lead]


def image_kernel(back_ref, message_ref, held_ref, scale_ref, turned_ref, image_ref, inner_ref):
    rows = image_ref.shape[1]
    width = turned_ref.shape[0] // back_ref.shape[0]
    own_other = message_ref[:, rows : 2 * rows]
    image = scale_ref[...] * project(back_ref, turned_ref, width) + damping * own_other
    image_ref[...] = image
    inner_ref[...] = row_product(image, held_ref[:, rows : 2 * rows])


def first_kernel(width, back_ref, held_ref, solved_ref, terms_ref, both_ref):
    queries = held_ref.shape[0]
    rows = terms_ref.shape[0]
    parts = range(back_ref.shape[0])
    one, two = (
        jnp.concatenate([back_ref[k, :, width + n * queries : width + (n + 1) * queries] for k in parts])
        for n in range(2)
    )
    step = held_ref[:, 2 * rows :]
    per_step = 1.0 / step
    lower, after, corner, same = masks(queries)
    eye = jnp.where(same, 1.0, 0.0)
    one_t, two_t = one.T, two.T
    bb = jnp.where(lower, one, one_t)
    tt = jnp.where(lower, one_t, one)
    tt = jnp.where(same, jnp.sum(jnp.where(after, two, 0.0), axis=1, keepdims=True), tt)
    plain = jnp.logical_or(jnp.logical_and(lower, jnp.logical_not(after)), corner)
    bab = jnp.where(plain, two, two_t)

    tb = bb - step * bab
    bat = per_step * (tb.T - tt)
    tab = bat.T
    inv = inverse_spd(bab, eye, both_ref)
    alpha = solve_with(bab, inv, bb)
    second = per_step * alpha
    fresh = product(second.T, tb - full(tab, alpha))
    mixed = -solve_with(bab, inv, product(bat, second))
    for k, mat in enumerate([alpha, second, fresh, mixed, product(tab, mixed)]):
        solved_ref[k] = mat
    for k in range(2):
        high, low = halves(held_ref[:, k * rows : (k + 1) * rows].T)
        for n, term in enumerate([high, low, high]):
            terms_ref[:, (3 * k + n) * queries : (3 * k + n + 1) * queries] = term


def finish_kernel(
    held_ref, solved_ref, terms_ref, late_ref, solution_hbm, residual_hbm, both_ref, out_ref, sems
):
    queries = held_ref.shape[0]
    rows = terms_ref.shape[0]
    tat = late_ref[:, rows:]
    per_step = 1.0 / held_ref[:, 2 * rows :]
    alpha, second, fresh, mixed, lead = (solved_ref[k] for k in range(5))
    shape = (queries, queries)
    row_id = lax.broadcasted_iota(jnp.int32, shape, 0)
    eye = jnp.where(row_id == lax.broadcasted_iota(jnp.int32, shape, 1), 1.0, 0.0)
    curv = product(second.T, lead + product(tat, second))
    curv = 0.5 * (curv + curv.T)
    high, low = halves(late_ref[:, :rows].T)
    image = jnp.concatenate([high, low, high], axis=1)
    inv = inverse_spd(curv, eye, both_ref)
    alpha_next = solve_with(curv, inv, fresh)
    gain = product(jnp.concatenate([mixed, second]), alpha_next)
    gain, gain_other = gain[:queries], gain[queries:]
    shift = per_step * gain
    weights = []
    for pair in (
        (alpha + gain, eye - second - shift),
        (gain_other, second + shift),
        (jnp.zeros(shape, jnp.float32), -gain_other),
    ):
        high, low = halves(jnp.concatenate(pair, axis=1))
        weights += [high, high, low]
    weights = jnp.concatenate(weights)
    copies = []
    step = rows // 2
    for k in range(2):
        block = pl.ds(k * step, step)
        terms = jnp.concatenate([terms_ref[block], image[k * step : (k + 1) * step]], axis=1)
        out_ref[block] = jnp.dot(terms, weights, preferred_element_type=jnp.float32)
        for n, target in enumerate([solution_hbm, residual_hbm]):
            source = out_ref.at[block, pl.ds(n * queries, queries)]
            copies.append(pltpu.make_async_copy(source, target.at[block], sems.at[2 * k + n]))
            copies[-1].start()
    for copy in copies:
        copy.wait()


def call(kernel, shapes, *args, scratch=(), dtypes=(jnp.float32, jnp.float32), out_space=pltpu.VMEM):
    outs = pl.pallas_call(
        kernel,
        out_shape=tuple(jax.ShapeDtypeStruct(*shape) for shape in zip(shapes, dtypes)),
        in_specs=[pl.BlockSpec(memory_space=pltpu.VMEM if near else pl.ANY) for near, _ in map(place, args)],
        out_specs=tuple(pl.BlockSpec(memory_space=out_space) for _ in shapes),
        scratch_shapes=scratch,
        compiler_params=pltpu.CompilerParams(vmem_limit_bytes=2**23),
    )(*(value for _, value in map(place, args)))
    return outs if len(outs) > 1 else outs[0]


class Far:
    def __init__(self, value):
        self.value = value


def place(arg):
    if isinstance(arg, Far):
        return False, pltpu.with_memory_space_constraint(arg.value, pltpu.MemorySpace.HBM)
    return True, arg


def on_device(rows_n, cols_n, grads, seeds, bank, query_ids):
    rows, depth = grads.shape
    queries = query_ids.shape[0]
    mine = queries // cols_n
    lanes = 128
    pieces = (rows_n, mine, depth // rows_n)

    def reduce_row(part):
        total = call(sum_kernel, [part.shape], swap(part, "row"), dtypes=[part.dtype])
        return swap(total, "row")

    seeds = seeds.reshape(-1, lanes)
    picked, scale = call(
        pick_kernel,
        [pieces, (1, rows)],
        Far(query_ids),
        Far(seeds),
        Far(bank),
        scratch=[
            pltpu.SMEM(query_ids.shape, jnp.int32),
            pltpu.VMEM(seeds.shape, jnp.int32),
            pltpu.VMEM(bank.shape, bank.dtype),
            pltpu.SemaphoreType.DMA((3,)),
        ],
        dtypes=[bank.dtype, jnp.float32],
    )
    chosen = reduce_row(picked)
    base, part, grads, turned = call(
        base_kernel,
        [(mine, rows), pieces, grads.shape, (depth, rows)],
        chosen,
        scale,
        Far(grads),
        scratch=[pltpu.SemaphoreType.DMA((rows_n,))],
        dtypes=[jnp.float32, jnp.float32, grads.dtype, grads.dtype],
    )
    back = reduce_row(part)
    wide = 2 * rows + lanes
    message, part = call(other_kernel, [(mine, wide), pieces], back, chosen, base, scale, grads, turned)
    held = spread(message, "col", cols_n).reshape(queries, wide)
    width = pieces[2]
    back = reduce_row(call(join_kernel, [(rows_n, mine, width + 2 * queries)], part, held))
    image, inner = call(
        image_kernel, [(mine, rows), (mine, queries)], back, message, held, scale, turned
    )
    both = pltpu.VMEM((2 * queries, queries), jnp.float32)
    solved, terms = call(
        functools.partial(first_kernel, width),
        [(5, queries, queries), (rows, 6 * queries)],
        back,
        held,
        scratch=[both],
        dtypes=[jnp.float32, jnp.bfloat16],
    )
    late = (cols_n, mine, rows + queries)
    inner = spread(inner, "row", rows_n)
    late = call(late_kernel, [late], inner, image)
    late = swap(late, "col")
    return call(
        finish_kernel,
        [(rows, queries), (rows, queries)],
        held,
        solved,
        terms,
        late.reshape(queries, rows + queries),
        scratch=[both, pltpu.VMEM((rows, 2 * queries), jnp.float32), pltpu.SemaphoreType.DMA((4,))],
        out_space=pl.ANY,
    )


def solution(mesh):
    placed = (P("row", None), P(), P("row", None), P())

    def body(*args):
        return on_device(mesh.shape["row"], mesh.shape["col"], *args)

    return jax.shard_map(
        body,
        mesh=mesh,
        in_specs=placed,
        out_specs=(P("row", None), P("row", None)),
        check_vma=False,
    )
```

```python
import functools

import jax
import jax.numpy as jnp
from jax import lax
from jax.experimental import pallas as pl
from jax.experimental.pallas import tpu as pltpu
from jax.sharding import PartitionSpec as P


damping = 0.5


def full(left, right):
    return lax.dot_general(
        left,
        right,
        (((1,), (0,)), ((), ())),
        precision=lax.Precision.HIGHEST,
        preferred_element_type=jnp.float32,
    )


def two_terms(value):
    high = value.astype(jnp.bfloat16).astype(jnp.float32)
    return jnp.concatenate([high, value - high]).astype(jnp.bfloat16)


def both_terms(product):
    half = product.shape[0] // 2
    return product[:half] + product[half:]


def bf16_dot(left, right, right_dim):
    return lax.dot_general(
        left, right, (((1,), (right_dim,)), ((), ())), preferred_element_type=jnp.float32
    )


def halves(value):
    high = value.astype(jnp.bfloat16)
    return high, (value - high.astype(jnp.float32)).astype(jnp.bfloat16)


def product(left, right):
    high, low = halves(right)
    top = jnp.concatenate([high, low], axis=1)
    bottom = jnp.concatenate([high, jnp.zeros_like(low)], axis=1)
    both = jnp.dot(
        jnp.concatenate(halves(left), axis=1),
        jnp.concatenate([top, bottom], axis=0),
        preferred_element_type=jnp.float32,
    )
    columns = right.shape[1]
    return both[:, :columns] + both[:, columns:]


def row_product(left, right):
    high, low = halves(right)
    rows = right.shape[0]
    both = bf16_dot(
        jnp.concatenate(halves(left), axis=1),
        jnp.concatenate(
            [
                jnp.concatenate([high, high], axis=1),
                jnp.concatenate([low, jnp.zeros_like(low)], axis=1),
            ]
        ),
        1,
    )
    return both[:, :rows] + both[:, rows:]


def swap(pieces, axis):
    return lax.all_to_all(pieces, axis, 0, 0, tiled=True)


def spread(piece, axis, size):
    return swap(jnp.broadcast_to(piece[None], (size,) + piece.shape), axis)


def inverse_spd(mat, eye, both_ref):
    size = mat.shape[0]
    on_diag = mat * eye
    across = lax.rsqrt(jnp.sum(on_diag, axis=0, keepdims=True))
    down = lax.rsqrt(jnp.sum(on_diag, axis=1, keepdims=True))
    unit = mat * across * down
    twice = product(unit, unit)
    reach = jnp.sum(jnp.abs(twice), axis=1, keepdims=True)
    share = 1.8 * lax.rsqrt(jnp.max(reach, axis=0, keepdims=True))
    part = share * unit
    inv = share * (2.0 * eye - part)
    left = eye - 2.0 * part + share * share * twice

    def advance(inv, left):
        both = product(jnp.concatenate([inv, left]), left)
        return inv + both[:size], both[size:]

    for _ in range(3):
        inv, left = advance(inv, left)
    both_ref[:size] = inv
    both_ref[size:] = left

    def open_still(state):
        count, remainder = state
        return jnp.logical_and(count < 40, remainder > 3e-4)

    def again(state):
        inv, left = advance(both_ref[:size], both_ref[size:])
        both_ref[:size] = inv
        both_ref[size:] = left
        return state[0] + 1, jnp.sum(left * left)

    lax.while_loop(open_still, again, (0, jnp.sum(left * left)))
    inv = both_ref[:size]
    inv = inv + product(inv, both_ref[size:])
    return inv * across * down


def solve_with(mat, inv, right):
    first = product(inv, right)
    return first + product(inv, right - full(mat, first))


def pick_kernel(
    ids_hbm,
    seeds_hbm,
    bank_hbm,
    grads_hbm,
    picked_ref,
    scale_ref,
    begin_ref,
    ids_ref,
    seeds_ref,
    bank_ref,
    sems,
):
    begin_hbm = grads_hbm.at[:, pl.ds(0, begin_ref.shape[1])]
    copies = [
        pltpu.make_async_copy(source, target, sems.at[k])
        for k, (source, target) in enumerate(
            [
                (ids_hbm, ids_ref),
                (bank_hbm, bank_ref),
                (seeds_hbm, seeds_ref),
                (begin_hbm, begin_ref),
            ]
        )
    ]
    for copy in copies:
        copy.start()
    parts, mine, width = picked_ref.shape
    bank_rows = bank_ref.shape[0]
    my_row = lax.axis_index("row")
    my_col = lax.axis_index("col")
    query = lax.broadcasted_iota(jnp.int32, (mine, bank_rows), 0)
    held = lax.broadcasted_iota(jnp.int32, (mine, bank_rows), 1)
    chosen = jnp.zeros((mine, bank_rows), jnp.bool_)
    copies[0].wait()
    for q in range(mine):
        local = ids_ref[my_col * mine + q] - my_row * bank_rows
        chosen = jnp.logical_or(chosen, jnp.logical_and(query == q, held == local))
    selector = jnp.where(chosen, 1.0, 0.0).astype(jnp.bfloat16)
    copies[1].wait()
    for k in range(parts):
        picked = bf16_dot(selector, bank_ref[:, k * width : (k + 1) * width], 0)
        picked_ref[k] = picked.astype(jnp.bfloat16)
    lanes = seeds_ref.shape[1]
    groups = scale_ref.shape[1] // lanes
    copies[2].wait()
    for k in range(groups):
        seeds = seeds_ref[pl.ds(my_row * groups + k, 1), :]
        scale_ref[:, k * lanes : (k + 1) * lanes] = jnp.exp2(seeds.astype(jnp.float32) / 4.0)
    copies[3].wait()


def sum_kernel(parts_ref, out_ref):
    total = parts_ref[0].astype(jnp.float32)
    for k in range(1, parts_ref.shape[0]):
        total += parts_ref[k].astype(jnp.float32)
    for k in range(out_ref.shape[0]):
        out_ref[k] = total.astype(out_ref.dtype)


def late_kernel(parts_ref, image_ref, out_ref):
    total = parts_ref[0]
    for k in range(1, parts_ref.shape[0]):
        total += parts_ref[k]
    late = jnp.concatenate([image_ref[...], total], axis=1)
    for k in range(out_ref.shape[0]):
        out_ref[k] = late


def partial_back(value, grads_ref, part_ref):
    terms = two_terms(value)
    parts, _, width = part_ref.shape
    for k in range(parts):
        product = bf16_dot(terms, grads_ref[:, k * width : (k + 1) * width], 0)
        part_ref[k] = both_terms(product)


def base_kernel(
    chosen_ref, scale_ref, begin_ref, grads_hbm, base_ref, part_ref, grads_ref, turned_ref, sems
):
    parts, _, width = chosen_ref.shape
    copies = []
    for k in range(parts):
        block = (slice(None), pl.ds(k * width, width))
        copies.append(pltpu.make_async_copy(grads_hbm.at[block], grads_ref.at[block], sems.at[k]))
    for copy in copies[1:] + copies[:1]:
        copy.start()
    total = jnp.zeros(base_ref.shape, jnp.float32)
    for k in range(parts):
        if k == 0:
            turned = begin_ref[...].T
        else:
            copies[k].wait()
            turned = grads_ref[:, k * width : (k + 1) * width].T
        turned_ref[k * width : (k + 1) * width] = turned
        total += bf16_dot(chosen_ref[k], turned, 0)
    copies[0].wait()
    scale = scale_ref[...]
    base = scale * total
    base_ref[...] = base
    partial_back(scale * base, grads_ref, part_ref)


def project(back_ref, turned_ref, width):
    parts, lead, _ = back_ref.shape
    total = jnp.zeros((2 * lead, turned_ref.shape[1]), jnp.float32)
    for k in range(parts):
        terms = two_terms(back_ref[k, :, :width])
        total += bf16_dot(terms, turned_ref[k * width : (k + 1) * width], 0)
    return both_terms(total)


def other_kernel(
    back_ref, chosen_ref, base_ref, scale_ref, grads_ref, turned_ref, message_ref, part_ref
):
    parts, lead, width = back_ref.shape
    rows = base_ref.shape[1]
    square = jnp.zeros((lead, width), jnp.float32)
    curve = jnp.zeros((lead, width), jnp.float32)
    for k in range(parts):
        back = back_ref[k]
        square += chosen_ref[k].astype(jnp.float32) * back
        curve += back * back
    square = jnp.sum(square, axis=1, keepdims=True)
    curve = jnp.sum(curve, axis=1, keepdims=True)
    step = square / (curve + damping * square)
    base = base_ref[...]
    scale = scale_ref[...]
    other = base - step * (scale * project(back_ref, turned_ref, width) + damping * base)
    message_ref[:, :rows] = base
    message_ref[:, rows : 2 * rows] = other
    message_ref[:, 2 * rows :] = jnp.broadcast_to(step, (lead, message_ref.shape[1] - 2 * rows))
    partial_back(scale * other, grads_ref, part_ref)


def masks(size):
    row = lax.broadcasted_iota(jnp.int32, (size, size), 0)
    column = lax.broadcasted_iota(jnp.int32, (size, size), 1)
    after = jnp.logical_or(column == row + 1, row == column + size - 1)
    return column <= row, after, column == row + size - 1, column == row


def join_kernel(part_ref, held_ref, out_ref):
    parts, lead, width = part_ref.shape
    rows = (held_ref.shape[1] - 128) // 2
    queries = held_ref.shape[0]
    stacked = jnp.concatenate([held_ref[:, :rows], held_ref[:, rows : 2 * rows]])
    square = row_product(stacked, stacked)
    bb, tb, tt = square[:queries, :queries], square[queries:, :queries], square[queries:, queries:]
    lower, after, corner, eye = masks(queries)
    bab = 1.0 / held_ref[:, 2 * rows :] * (bb - tb)
    on_diag = jnp.sum(jnp.where(eye, tt, 0.0), axis=1, keepdims=True)
    inner = [
        jnp.where(lower, bb, tt),
        jnp.where(after, on_diag, jnp.where(jnp.logical_or(lower, corner), bab, 0.0)),
    ]
    for k in range(parts):
        out_ref[k, :, :width] = part_ref[k]
        for n, mat in enumerate(inner):
            lanes = slice(width + n * mat.shape[1], width + (n + 1) * mat.shape[1])
            out_ref[k, :, lanes] = mat[k * lead : (k + 1) * lead]


def image_kernel(back_ref, message_ref, held_ref, scale_ref, turned_ref, image_ref, inner_ref):
    rows = image_ref.shape[1]
    width = turned_ref.shape[0] // back_ref.shape[0]
    own_other = message_ref[:, rows : 2 * rows]
    image = scale_ref[...] * project(back_ref, turned_ref, width) + damping * own_other
    image_ref[...] = image
    inner_ref[...] = row_product(image, held_ref[:, rows : 2 * rows])


def first_kernel(width, back_ref, held_ref, solved_ref, terms_ref, both_ref):
    queries = held_ref.shape[0]
    rows = terms_ref.shape[0]
    parts = range(back_ref.shape[0])
    one, two = (
        jnp.concatenate([back_ref[k, :, width + n * queries : width + (n + 1) * queries] for k in parts])
        for n in range(2)
    )
    step = held_ref[:, 2 * rows :]
    per_step = 1.0 / step
    lower, after, corner, same = masks(queries)
    eye = jnp.where(same, 1.0, 0.0)
    one_t, two_t = one.T, two.T
    bb = jnp.where(lower, one, one_t)
    tt = jnp.where(lower, one_t, one)
    tt = jnp.where(same, jnp.sum(jnp.where(after, two, 0.0), axis=1, keepdims=True), tt)
    plain = jnp.logical_or(jnp.logical_and(lower, jnp.logical_not(after)), corner)
    bab = jnp.where(plain, two, two_t)

    tb = bb - step * bab
    bat = per_step * (tb.T - tt)
    tab = bat.T
    inv = inverse_spd(bab, eye, both_ref)
    alpha = solve_with(bab, inv, bb)
    second = per_step * alpha
    second_t = second.T
    fresh = product(second_t, tb - full(tab, alpha))
    mixed = -solve_with(bab, inv, product(bat, second))
    for k, mat in enumerate([alpha, second, second_t, fresh, mixed, product(tab, mixed)]):
        solved_ref[k] = mat
    for k in range(2):
        high, low = halves(held_ref[:, k * rows : (k + 1) * rows].T)
        for n, term in enumerate([high, low, high]):
            terms_ref[:, (3 * k + n) * queries : (3 * k + n + 1) * queries] = term


def finish_kernel(
    held_ref, solved_ref, terms_ref, late_ref, solution_hbm, residual_hbm, both_ref, out_ref, sems
):
    queries = held_ref.shape[0]
    rows = terms_ref.shape[0]
    tat = late_ref[:, rows:]
    per_step = 1.0 / held_ref[:, 2 * rows :]
    alpha, second, second_t, fresh, mixed, lead = (solved_ref[k] for k in range(6))
    shape = (queries, queries)
    row_id = lax.broadcasted_iota(jnp.int32, shape, 0)
    eye = jnp.where(row_id == lax.broadcasted_iota(jnp.int32, shape, 1), 1.0, 0.0)
    curv = product(second_t, lead + product(tat, second))
    high, low = halves(late_ref[:, :rows].T)
    image = jnp.concatenate([high, low, high], axis=1)
    inv = inverse_spd(curv, eye, both_ref)
    alpha_next = solve_with(curv, inv, fresh)
    gain = product(jnp.concatenate([mixed, second]), alpha_next)
    gain, gain_other = gain[:queries], gain[queries:]
    shift = per_step * gain
    weights = []
    for pair in (
        (alpha + gain, eye - second - shift),
        (gain_other, second + shift),
        (jnp.zeros(shape, jnp.float32), -gain_other),
    ):
        high, low = halves(jnp.concatenate(pair, axis=1))
        weights += [high, high, low]
    weights = jnp.concatenate(weights)
    copies = []
    step = rows // 2
    for k in range(2):
        block = pl.ds(k * step, step)
        terms = jnp.concatenate([terms_ref[block], image[k * step : (k + 1) * step]], axis=1)
        out_ref[block] = jnp.dot(terms, weights, preferred_element_type=jnp.float32)
        for n, target in enumerate([solution_hbm, residual_hbm]):
            source = out_ref.at[block, pl.ds(n * queries, queries)]
            copies.append(pltpu.make_async_copy(source, target.at[block], sems.at[2 * k + n]))
            copies[-1].start()
    for copy in copies:
        copy.wait()


def call(kernel, shapes, *args, scratch=(), dtypes=(jnp.float32, jnp.float32), out_space=pltpu.VMEM):
    outs = pl.pallas_call(
        kernel,
        out_shape=tuple(jax.ShapeDtypeStruct(*shape) for shape in zip(shapes, dtypes)),
        in_specs=[pl.BlockSpec(memory_space=pltpu.VMEM if near else pl.ANY) for near, _ in map(place, args)],
        out_specs=tuple(pl.BlockSpec(memory_space=out_space) for _ in shapes),
        scratch_shapes=scratch,
        compiler_params=pltpu.CompilerParams(vmem_limit_bytes=2**23),
    )(*(value for _, value in map(place, args)))
    return outs if len(outs) > 1 else outs[0]


class Far:
    def __init__(self, value):
        self.value = value


def place(arg):
    if isinstance(arg, Far):
        return False, pltpu.with_memory_space_constraint(arg.value, pltpu.MemorySpace.HBM)
    return True, arg


def on_device(rows_n, cols_n, grads, seeds, bank, query_ids):
    rows, depth = grads.shape
    queries = query_ids.shape[0]
    mine = queries // cols_n
    lanes = 128
    pieces = (rows_n, mine, depth // rows_n)

    def reduce_row(part):
        total = call(sum_kernel, [part.shape], swap(part, "row"), dtypes=[part.dtype])
        return swap(total, "row")

    seeds = seeds.reshape(-1, lanes)
    picked, scale, begin = call(
        pick_kernel,
        [pieces, (1, rows), (rows, pieces[2])],
        Far(query_ids),
        Far(seeds),
        Far(bank),
        Far(grads),
        scratch=[
            pltpu.SMEM(query_ids.shape, jnp.int32),
            pltpu.VMEM(seeds.shape, jnp.int32),
            pltpu.VMEM(bank.shape, bank.dtype),
            pltpu.SemaphoreType.DMA((4,)),
        ],
        dtypes=[bank.dtype, jnp.float32, grads.dtype],
    )
    chosen = reduce_row(picked)
    base, part, grads, turned = call(
        base_kernel,
        [(mine, rows), pieces, grads.shape, (depth, rows)],
        chosen,
        scale,
        begin,
        Far(grads),
        scratch=[pltpu.SemaphoreType.DMA((rows_n,))],
        dtypes=[jnp.float32, jnp.float32, grads.dtype, grads.dtype],
    )
    back = reduce_row(part)
    wide = 2 * rows + lanes
    message, part = call(other_kernel, [(mine, wide), pieces], back, chosen, base, scale, grads, turned)
    held = spread(message, "col", cols_n).reshape(queries, wide)
    width = pieces[2]
    back = reduce_row(call(join_kernel, [(rows_n, mine, width + 2 * queries)], part, held))
    image, inner = call(
        image_kernel, [(mine, rows), (mine, queries)], back, message, held, scale, turned
    )
    both = pltpu.VMEM((2 * queries, queries), jnp.float32)
    solved, terms = call(
        functools.partial(first_kernel, width),
        [(6, queries, queries), (rows, 6 * queries)],
        back,
        held,
        scratch=[both],
        dtypes=[jnp.float32, jnp.bfloat16],
    )
    late = (cols_n, mine, rows + queries)
    inner = spread(inner, "row", rows_n)
    late = call(late_kernel, [late], inner, image)
    late = swap(late, "col")
    return call(
        finish_kernel,
        [(rows, queries), (rows, queries)],
        held,
        solved,
        terms,
        late.reshape(queries, rows + queries),
        scratch=[both, pltpu.VMEM((rows, 2 * queries), jnp.float32), pltpu.SemaphoreType.DMA((4,))],
        out_space=pl.ANY,
    )


def solution(mesh):
    placed = (P("row", None), P(), P("row", None), P())

    def body(*args):
        return on_device(mesh.shape["row"], mesh.shape["col"], *args)

    return jax.shard_map(
        body,
        mesh=mesh,
        in_specs=placed,
        out_specs=(P("row", None), P("row", None)),
        check_vma=False,
    )
```

```python
import functools

import jax
import jax.numpy as jnp
from jax import lax
from jax.experimental import pallas as pl
from jax.experimental.pallas import tpu as pltpu
from jax.sharding import PartitionSpec as P


damping = 0.5


def full(left, right):
    return lax.dot_general(
        left,
        right,
        (((1,), (0,)), ((), ())),
        precision=lax.Precision.HIGHEST,
        preferred_element_type=jnp.float32,
    )


def two_terms(value):
    high = value.astype(jnp.bfloat16).astype(jnp.float32)
    return jnp.concatenate([high, value - high]).astype(jnp.bfloat16)


def both_terms(product):
    half = product.shape[0] // 2
    return product[:half] + product[half:]


def bf16_dot(left, right, right_dim):
    return lax.dot_general(
        left, right, (((1,), (right_dim,)), ((), ())), preferred_element_type=jnp.float32
    )


def halves(value):
    high = value.astype(jnp.bfloat16)
    return high, (value - high.astype(jnp.float32)).astype(jnp.bfloat16)


def product(left, right):
    high, low = halves(right)
    top = jnp.concatenate([high, low], axis=1)
    bottom = jnp.concatenate([high, jnp.zeros_like(low)], axis=1)
    both = jnp.dot(
        jnp.concatenate(halves(left), axis=1),
        jnp.concatenate([top, bottom], axis=0),
        preferred_element_type=jnp.float32,
    )
    columns = right.shape[1]
    return both[:, :columns] + both[:, columns:]


def row_product(left, right):
    high, low = halves(right)
    rows = right.shape[0]
    both = bf16_dot(
        jnp.concatenate(halves(left), axis=1),
        jnp.concatenate(
            [
                jnp.concatenate([high, high], axis=1),
                jnp.concatenate([low, jnp.zeros_like(low)], axis=1),
            ]
        ),
        1,
    )
    return both[:, :rows] + both[:, rows:]


def swap(pieces, axis):
    return lax.all_to_all(pieces, axis, 0, 0, tiled=True)


def spread(piece, axis, size):
    return swap(jnp.broadcast_to(piece[None], (size,) + piece.shape), axis)


def inverse_spd(mat, eye, both_ref):
    size = mat.shape[0]
    on_diag = mat * eye
    across = lax.rsqrt(jnp.sum(on_diag, axis=0, keepdims=True))
    down = lax.rsqrt(jnp.sum(on_diag, axis=1, keepdims=True))
    unit = mat * across * down
    twice = product(unit, unit)
    reach = jnp.sum(jnp.abs(twice), axis=1, keepdims=True)
    share = 1.8 * lax.rsqrt(jnp.max(reach, axis=0, keepdims=True))
    part = share * unit
    inv = share * (2.0 * eye - part)
    left = eye - 2.0 * part + share * share * twice

    def advance(inv, left):
        both = product(jnp.concatenate([inv, left]), left)
        return inv + both[:size], both[size:]

    for _ in range(3):
        inv, left = advance(inv, left)
    both_ref[:size] = inv
    both_ref[size:] = left

    def open_still(state):
        count, remainder = state
        return jnp.logical_and(count < 40, remainder > 3e-4)

    def again(state):
        inv, left = advance(both_ref[:size], both_ref[size:])
        both_ref[:size] = inv
        both_ref[size:] = left
        return state[0] + 1, jnp.sum(left * left)

    lax.while_loop(open_still, again, (0, jnp.sum(left * left)))
    inv = both_ref[:size]
    inv = inv + product(inv, both_ref[size:])
    return inv * across * down


def solve_with(mat, inv, right):
    first = product(inv, right)
    return first + product(inv, right - full(mat, first))


def pick_kernel(
    ids_hbm,
    seeds_hbm,
    bank_hbm,
    grads_hbm,
    picked_ref,
    scale_ref,
    begin_ref,
    ids_ref,
    seeds_ref,
    bank_ref,
    sems,
):
    begin_hbm = grads_hbm.at[:, pl.ds(0, begin_ref.shape[1])]
    copies = [
        pltpu.make_async_copy(source, target, sems.at[k])
        for k, (source, target) in enumerate(
            [
                (ids_hbm, ids_ref),
                (bank_hbm, bank_ref),
                (seeds_hbm, seeds_ref),
                (begin_hbm, begin_ref),
            ]
        )
    ]
    for copy in copies:
        copy.start()
    parts, mine, width = picked_ref.shape
    bank_rows = bank_ref.shape[0]
    my_row = lax.axis_index("row")
    my_col = lax.axis_index("col")
    query = lax.broadcasted_iota(jnp.int32, (mine, bank_rows), 0)
    held = lax.broadcasted_iota(jnp.int32, (mine, bank_rows), 1)
    chosen = jnp.zeros((mine, bank_rows), jnp.bool_)
    copies[0].wait()
    for q in range(mine):
        local = ids_ref[my_col * mine + q] - my_row * bank_rows
        chosen = jnp.logical_or(chosen, jnp.logical_and(query == q, held == local))
    selector = jnp.where(chosen, 1.0, 0.0).astype(jnp.bfloat16)
    copies[1].wait()
    for k in range(parts):
        picked = bf16_dot(selector, bank_ref[:, k * width : (k + 1) * width], 0)
        picked_ref[k] = picked.astype(jnp.bfloat16)
    lanes = seeds_ref.shape[1]
    groups = scale_ref.shape[1] // lanes
    copies[2].wait()
    for k in range(groups):
        seeds = seeds_ref[pl.ds(my_row * groups + k, 1), :]
        scale_ref[:, k * lanes : (k + 1) * lanes] = jnp.exp2(seeds.astype(jnp.float32) / 4.0)
    copies[3].wait()


def sum_kernel(parts_ref, out_ref):
    total = parts_ref[0].astype(jnp.float32)
    for k in range(1, parts_ref.shape[0]):
        total += parts_ref[k].astype(jnp.float32)
    for k in range(out_ref.shape[0]):
        out_ref[k] = total.astype(out_ref.dtype)


def late_kernel(parts_ref, image_ref, out_ref):
    total = parts_ref[0]
    for k in range(1, parts_ref.shape[0]):
        total += parts_ref[k]
    late = jnp.concatenate([image_ref[...], total], axis=1)
    for k in range(out_ref.shape[0]):
        out_ref[k] = late


def partial_back(value, grads_ref, part_ref):
    terms = two_terms(value)
    parts, _, width = part_ref.shape
    for k in range(parts):
        product = bf16_dot(terms, grads_ref[:, k * width : (k + 1) * width], 0)
        part_ref[k] = both_terms(product)


def base_kernel(
    chosen_ref, scale_ref, begin_ref, grads_hbm, base_ref, part_ref, grads_ref, turned_ref, sems
):
    parts, _, width = chosen_ref.shape
    copies = []
    for k in range(parts):
        block = (slice(None), pl.ds(k * width, width))
        copies.append(pltpu.make_async_copy(grads_hbm.at[block], grads_ref.at[block], sems.at[k]))
    ready = begin_ref.shape[1] // width
    for copy in copies[ready:] + copies[:ready]:
        copy.start()
    total = jnp.zeros(base_ref.shape, jnp.float32)
    for k in range(parts):
        if k < ready:
            turned = begin_ref[:, k * width : (k + 1) * width].T
        else:
            copies[k].wait()
            turned = grads_ref[:, k * width : (k + 1) * width].T
        turned_ref[k * width : (k + 1) * width] = turned
        total += bf16_dot(chosen_ref[k], turned, 0)
    for copy in copies[:ready]:
        copy.wait()
    scale = scale_ref[...]
    base = scale * total
    base_ref[...] = base
    partial_back(scale * base, grads_ref, part_ref)


def project(back_ref, turned_ref, width):
    parts, lead, _ = back_ref.shape
    total = jnp.zeros((2 * lead, turned_ref.shape[1]), jnp.float32)
    for k in range(parts):
        terms = two_terms(back_ref[k, :, :width])
        total += bf16_dot(terms, turned_ref[k * width : (k + 1) * width], 0)
    return both_terms(total)


def other_kernel(
    back_ref, chosen_ref, base_ref, scale_ref, grads_ref, turned_ref, message_ref, part_ref
):
    parts, lead, width = back_ref.shape
    rows = base_ref.shape[1]
    square = jnp.zeros((lead, width), jnp.float32)
    curve = jnp.zeros((lead, width), jnp.float32)
    for k in range(parts):
        back = back_ref[k]
        square += chosen_ref[k].astype(jnp.float32) * back
        curve += back * back
    square = jnp.sum(square, axis=1, keepdims=True)
    curve = jnp.sum(curve, axis=1, keepdims=True)
    step = square / (curve + damping * square)
    base = base_ref[...]
    scale = scale_ref[...]
    other = base - step * (scale * project(back_ref, turned_ref, width) + damping * base)
    message_ref[:, :rows] = base
    message_ref[:, rows : 2 * rows] = other
    message_ref[:, 2 * rows :] = jnp.broadcast_to(step, (lead, message_ref.shape[1] - 2 * rows))
    partial_back(scale * other, grads_ref, part_ref)


def masks(size):
    row = lax.broadcasted_iota(jnp.int32, (size, size), 0)
    column = lax.broadcasted_iota(jnp.int32, (size, size), 1)
    after = jnp.logical_or(column == row + 1, row == column + size - 1)
    return column <= row, after, column == row + size - 1, column == row


def join_kernel(part_ref, held_ref, out_ref):
    parts, lead, width = part_ref.shape
    rows = (held_ref.shape[1] - 128) // 2
    queries = held_ref.shape[0]
    stacked = jnp.concatenate([held_ref[:, :rows], held_ref[:, rows : 2 * rows]])
    square = row_product(stacked, stacked)
    bb, tb, tt = square[:queries, :queries], square[queries:, :queries], square[queries:, queries:]
    lower, after, corner, eye = masks(queries)
    bab = 1.0 / held_ref[:, 2 * rows :] * (bb - tb)
    on_diag = jnp.sum(jnp.where(eye, tt, 0.0), axis=1, keepdims=True)
    inner = [
        jnp.where(lower, bb, tt),
        jnp.where(after, on_diag, jnp.where(jnp.logical_or(lower, corner), bab, 0.0)),
    ]
    for k in range(parts):
        out_ref[k, :, :width] = part_ref[k]
        for n, mat in enumerate(inner):
            lanes = slice(width + n * mat.shape[1], width + (n + 1) * mat.shape[1])
            out_ref[k, :, lanes] = mat[k * lead : (k + 1) * lead]


def image_kernel(back_ref, message_ref, held_ref, scale_ref, turned_ref, image_ref, inner_ref):
    rows = image_ref.shape[1]
    width = turned_ref.shape[0] // back_ref.shape[0]
    own_other = message_ref[:, rows : 2 * rows]
    image = scale_ref[...] * project(back_ref, turned_ref, width) + damping * own_other
    image_ref[...] = image
    inner_ref[...] = row_product(image, held_ref[:, rows : 2 * rows])


def first_kernel(width, back_ref, held_ref, solved_ref, terms_ref, both_ref):
    queries = held_ref.shape[0]
    rows = terms_ref.shape[0]
    parts = range(back_ref.shape[0])
    one, two = (
        jnp.concatenate([back_ref[k, :, width + n * queries : width + (n + 1) * queries] for k in parts])
        for n in range(2)
    )
    step = held_ref[:, 2 * rows :]
    per_step = 1.0 / step
    lower, after, corner, same = masks(queries)
    eye = jnp.where(same, 1.0, 0.0)
    one_t, two_t = one.T, two.T
    bb = jnp.where(lower, one, one_t)
    tt = jnp.where(lower, one_t, one)
    tt = jnp.where(same, jnp.sum(jnp.where(after, two, 0.0), axis=1, keepdims=True), tt)
    plain = jnp.logical_or(jnp.logical_and(lower, jnp.logical_not(after)), corner)
    bab = jnp.where(plain, two, two_t)

    tb = bb - step * bab
    bat = per_step * (tb.T - tt)
    tab = bat.T
    inv = inverse_spd(bab, eye, both_ref)
    alpha = solve_with(bab, inv, bb)
    second = per_step * alpha
    second_t = second.T
    fresh = product(second_t, tb - full(tab, alpha))
    mixed = -solve_with(bab, inv, product(bat, second))
    for k, mat in enumerate([alpha, second, second_t, fresh, mixed, product(tab, mixed)]):
        solved_ref[k] = mat
    for k in range(2):
        high, low = halves(held_ref[:, k * rows : (k + 1) * rows].T)
        for n, term in enumerate([high, low, high]):
            terms_ref[:, (3 * k + n) * queries : (3 * k + n + 1) * queries] = term


def finish_kernel(
    held_ref, solved_ref, terms_ref, late_ref, solution_hbm, residual_hbm, both_ref, out_ref, sems
):
    queries = held_ref.shape[0]
    rows = terms_ref.shape[0]
    tat = late_ref[:, rows:]
    per_step = 1.0 / held_ref[:, 2 * rows :]
    alpha, second, second_t, fresh, mixed, lead = (solved_ref[k] for k in range(6))
    shape = (queries, queries)
    row_id = lax.broadcasted_iota(jnp.int32, shape, 0)
    eye = jnp.where(row_id == lax.broadcasted_iota(jnp.int32, shape, 1), 1.0, 0.0)
    curv = product(second_t, lead + product(tat, second))
    high, low = halves(late_ref[:, :rows].T)
    image = jnp.concatenate([high, low, high], axis=1)
    inv = inverse_spd(curv, eye, both_ref)
    alpha_next = solve_with(curv, inv, fresh)
    gain = product(jnp.concatenate([mixed, second]), alpha_next)
    gain, gain_other = gain[:queries], gain[queries:]
    shift = per_step * gain
    weights = []
    for pair in (
        (alpha + gain, eye - second - shift),
        (gain_other, second + shift),
        (jnp.zeros(shape, jnp.float32), -gain_other),
    ):
        high, low = halves(jnp.concatenate(pair, axis=1))
        weights += [high, high, low]
    weights = jnp.concatenate(weights)
    copies = []
    step = rows // 2
    for k in range(2):
        block = pl.ds(k * step, step)
        terms = jnp.concatenate([terms_ref[block], image[k * step : (k + 1) * step]], axis=1)
        out_ref[block] = jnp.dot(terms, weights, preferred_element_type=jnp.float32)
        for n, target in enumerate([solution_hbm, residual_hbm]):
            source = out_ref.at[block, pl.ds(n * queries, queries)]
            copies.append(pltpu.make_async_copy(source, target.at[block], sems.at[2 * k + n]))
            copies[-1].start()
    for copy in copies:
        copy.wait()


def call(kernel, shapes, *args, scratch=(), dtypes=(jnp.float32, jnp.float32), out_space=pltpu.VMEM):
    outs = pl.pallas_call(
        kernel,
        out_shape=tuple(jax.ShapeDtypeStruct(*shape) for shape in zip(shapes, dtypes)),
        in_specs=[pl.BlockSpec(memory_space=pltpu.VMEM if near else pl.ANY) for near, _ in map(place, args)],
        out_specs=tuple(pl.BlockSpec(memory_space=out_space) for _ in shapes),
        scratch_shapes=scratch,
        compiler_params=pltpu.CompilerParams(vmem_limit_bytes=2**23),
    )(*(value for _, value in map(place, args)))
    return outs if len(outs) > 1 else outs[0]


class Far:
    def __init__(self, value):
        self.value = value


def place(arg):
    if isinstance(arg, Far):
        return False, pltpu.with_memory_space_constraint(arg.value, pltpu.MemorySpace.HBM)
    return True, arg


def on_device(rows_n, cols_n, grads, seeds, bank, query_ids):
    rows, depth = grads.shape
    queries = query_ids.shape[0]
    mine = queries // cols_n
    lanes = 128
    pieces = (rows_n, mine, depth // rows_n)

    def reduce_row(part):
        total = call(sum_kernel, [part.shape], swap(part, "row"), dtypes=[part.dtype])
        return swap(total, "row")

    seeds = seeds.reshape(-1, lanes)
    picked, scale, begin = call(
        pick_kernel,
        [pieces, (1, rows), (rows, 4 * pieces[2])],
        Far(query_ids),
        Far(seeds),
        Far(bank),
        Far(grads),
        scratch=[
            pltpu.SMEM(query_ids.shape, jnp.int32),
            pltpu.VMEM(seeds.shape, jnp.int32),
            pltpu.VMEM(bank.shape, bank.dtype),
            pltpu.SemaphoreType.DMA((4,)),
        ],
        dtypes=[bank.dtype, jnp.float32, grads.dtype],
    )
    chosen = reduce_row(picked)
    base, part, grads, turned = call(
        base_kernel,
        [(mine, rows), pieces, grads.shape, (depth, rows)],
        chosen,
        scale,
        begin,
        Far(grads),
        scratch=[pltpu.SemaphoreType.DMA((rows_n,))],
        dtypes=[jnp.float32, jnp.float32, grads.dtype, grads.dtype],
    )
    back = reduce_row(part)
    wide = 2 * rows + lanes
    message, part = call(other_kernel, [(mine, wide), pieces], back, chosen, base, scale, grads, turned)
    held = spread(message, "col", cols_n).reshape(queries, wide)
    width = pieces[2]
    back = reduce_row(call(join_kernel, [(rows_n, mine, width + 2 * queries)], part, held))
    image, inner = call(
        image_kernel, [(mine, rows), (mine, queries)], back, message, held, scale, turned
    )
    both = pltpu.VMEM((2 * queries, queries), jnp.float32)
    solved, terms = call(
        functools.partial(first_kernel, width),
        [(6, queries, queries), (rows, 6 * queries)],
        back,
        held,
        scratch=[both],
        dtypes=[jnp.float32, jnp.bfloat16],
    )
    late = (cols_n, mine, rows + queries)
    inner = spread(inner, "row", rows_n)
    late = call(late_kernel, [late], inner, image)
    late = swap(late, "col")
    return call(
        finish_kernel,
        [(rows, queries), (rows, queries)],
        held,
        solved,
        terms,
        late.reshape(queries, rows + queries),
        scratch=[both, pltpu.VMEM((rows, 2 * queries), jnp.float32), pltpu.SemaphoreType.DMA((4,))],
        out_space=pl.ANY,
    )


def solution(mesh):
    placed = (P("row", None), P(), P("row", None), P())

    def body(*args):
        return on_device(mesh.shape["row"], mesh.shape["col"], *args)

    return jax.shard_map(
        body,
        mesh=mesh,
        in_specs=placed,
        out_specs=(P("row", None), P("row", None)),
        check_vma=False,
    )
```
